128 devices in a mesh: grp: 4 (over y), dev: 32 (over x, z, core).
Axes of the slice: x: 4, y: 4, z: 4, core: 2. Of those that a mesh axis runs over, the one named last changes fastest.
Arguments:
- slab: float32 [4096, 64, 512], P(('grp', 'dev')), may hold values from -40 to 40
- start: float32 [512, 256], replicated, may hold values from -0.25 to 0.25
Outputs:
- next_unfolding: float32 [64, 4096, 256], P('dev', 'grp')
- basis: float32 [512, 256], replicated
The draws below stay inside these ranges and needn't reach their ends.
All inputs are finite; a program needn't handle non-finite values.
Results may differ from the reference program's by a relative error of at most 0.00023.
Values sent between devices are 32-bit elements; how exact they have to be, the bound alone decides.
A program may use at most 64 MiB of HBM per device.

```python
import math
import jax
import jax.numpy as jnp
from jax import lax

K = 512
RANK = 256
NB = 64
ITERS = 4
NA = 4096
ROWS = 262144


def draw_slab(key, part):
    first, second = jax.random.split(jax.random.fold_in(key, 11), 2)
    columns = jnp.exp(jax.random.uniform(second, (K,), jnp.float32, math.log(0.5), math.log(2.0)))
    rising = jnp.exp(math.log(3.0) * jnp.arange(NA, dtype=jnp.float32) / NA)[:, None, None]
    values = jax.random.truncated_normal(first, -6.0, 6.0, (NA, NB, K), jnp.float32)
    return values * columns * rising


def noise(own_key, extent, width, limit, kind=jnp.bfloat16):
    return jnp.clip(width * jax.random.normal(own_key, extent, jnp.float32), -limit, limit).astype(kind)


def setup_inputs(seed: int = 0) -> dict:
    streams_of = jax.random.split(jax.random.key(seed), 3)
    return {
        "slab": draw_slab(jax.random.fold_in(streams_of[2], 71), 0),
        "start": noise(streams_of[1], (K, RANK), K ** -0.5, 0.25, jnp.float32),
    }


def reference(slab, start):
    highest = lax.Precision.HIGHEST
    matrix = slab.reshape(ROWS, K)
    gram = jnp.dot(matrix.T, matrix, precision=highest) / jnp.float32(ROWS)
    basis = start
    for step in range(ITERS):
        product = jnp.dot(gram, basis, precision=highest)
        lower = jnp.linalg.cholesky(jnp.dot(product.T, product, precision=highest))
        basis = lax.linalg.triangular_solve(lower, product, left_side=False, lower=True, transpose_a=True)
    projected = jnp.einsum('abk,kr->bar', slab, basis, precision=highest)
    return (projected, basis)
```

```python
import jax
import jax.numpy as jnp
from jax import lax
from jax.experimental import pallas as pl
from jax.experimental.pallas import tpu as pltpu
from jax.sharding import Mesh
from jax.sharding import PartitionSpec as P

ITERS = 4
DEV = ("dev_0", "dev_1", "dev_2")
GRP_DEV = ("grp", "dev_0", "dev_1", "dev_2")


def in_blocks(shard, dim, peers):
    before, after = (shard.shape[:dim], shard.shape[dim + 1 :])
    return jnp.moveaxis(shard.reshape(*before, peers, -1, *after), dim, 0)


def summed_on_arrival(shard, axis, dim):
    peers = lax.axis_size(axis)
    blocks = lax.all_to_all(in_blocks(shard, dim, peers), axis, 0, 0, tiled=True)
    return jnp.sum(blocks, axis=0)


def sum_by_axis(shard, axes, dim):
    far, near = axes
    blocks = in_blocks(shard, dim, lax.axis_size(far))
    nearer = summed_on_arrival(blocks, near, dim + 1)
    arrived = lax.all_to_all(nearer, far, split_axis=0, concat_axis=0, tiled=True)
    return arrived.sum(axis=0)


def rows_for(lines, peers):
    spare = -lines.shape[0] % peers
    if not spare:
        return lines
    return jnp.concatenate([lines, jnp.zeros((spare, *lines.shape[1:]), lines.dtype)])


def copy_for_each(shard, axis):
    peers = lax.axis_size(axis)
    return lax.all_to_all(
        jnp.broadcast_to(shard[None], (peers, *shard.shape)), axis, 0, 0, tiled=True
    )


def laid_out(blocks, dim):
    shape = list(blocks.shape[1:])
    shape[dim] *= blocks.shape[0]
    return jnp.moveaxis(blocks, 0, dim).reshape(shape)


def gather_axes(shard, axes, dim):
    far, near = axes
    initial = copy_for_each(shard, far)
    blocks = jnp.swapaxes(copy_for_each(initial, near), 0, 1)
    return laid_out(blocks.reshape(-1, *shard.shape), dim)


def total_of(shard, axes):
    lines = shard.reshape(-1, shard.shape[-1])
    own = sum_by_axis(rows_for(lines, lax.axis_size(axes[0]) * lax.axis_size(axes[1])), axes, 0)
    whole = gather_axes(own, axes, 0)
    return whole[: len(lines)].reshape(shard.shape)


HIGHEST = lax.Precision.HIGHEST
BLOCK = 64


def contract(a, b, dim_a, dim_b):
    return lax.dot_general(
        a, b, (((dim_a,), (dim_b,)), ((), ())), precision=HIGHEST, preferred_element_type=jnp.float32
    )


def inverse_factor(block):
    size = block.shape[0]
    diagonal = lax.broadcasted_iota(jnp.int32, (size, size), 0) == lax.broadcasted_iota(jnp.int32, (size, size), 1)
    both = jnp.concatenate([block, diagonal.astype(jnp.float32)], axis=1)
    wide = (8, 2 * size)
    count = size // 8
    tiles = [both[8 * t : 8 * t + 8, :] for t in range(count)]
    row_of = lax.broadcasted_iota(jnp.int32, wide, 0)
    for t in range(count):
        cols = [[jnp.broadcast_to(tiles[u][:, 8 * t + c : 8 * t + c + 1], wide) for u in range(t, count)] for c in range(8)]
        rows = [jnp.broadcast_to(tiles[t][i : i + 1, :], wide) for i in range(8)]
        a = [
            [
                jnp.broadcast_to(jnp.sum(jnp.where(row_of == i, cols[c][0], 0.0), axis=0, keepdims=True), wide)
                if i >= c
                else None
                for c in range(8)
            ]
            for i in range(8)
        ]
        unit = [[None] * 8 for _ in range(8)]
        scaled = []
        for c in range(8):
            inverse = 1.0 / a[c][c]
            for i in range(c + 1, 8):
                unit[i][c] = a[i][c] * inverse
            for k in range(c + 1, 8):
                for i in range(k, 8):
                    a[i][k] = a[i][k] - unit[i][c] * a[k][c]
            for i in range(c + 1, 8):
                rows[i] = rows[i] - unit[i][c] * rows[c]
            scaled.append(rows[c] * inverse)
        for u in range(t + 1, count):
            col = [cols[c][u - t] for c in range(8)]
            for c in range(8):
                for k in range(c + 1, 8):
                    col[k] = col[k] - unit[k][c] * col[c]
            change = col[0] * scaled[0]
            for c in range(1, 8):
                change = change + col[c] * scaled[c]
            tiles[u] = tiles[u] - change
        for c in range(8):
            tiles[t] = jnp.where(row_of == c, rows[c] * lax.rsqrt(a[c][c]), tiles[t])
    return jnp.concatenate(tiles, axis=0)[:, size:]


def inverse_cholesky(m_ref, v_ref):
    size = m_ref.shape[0]
    v_ref[...] = jnp.zeros_like(v_ref)
    for lo in range(0, size, BLOCK):
        hi = lo + BLOCK
        inner = inverse_factor(m_ref[lo:hi, lo:hi])
        if lo:
            v_ref[lo:hi, :lo] = contract(inner, v_ref[lo:hi, :lo], 1, 0)
        v_ref[lo:hi, lo:hi] = inner
        if hi < size:
            across = contract(inner, m_ref[lo:hi, hi:], 1, 0)
            down = contract(m_ref[hi:, lo:hi], inner, 1, 1)
            m_ref[hi:, hi:] -= contract(down, across, 1, 0)
            v_ref[hi:, :hi] -= contract(down, v_ref[lo:hi, :hi], 1, 0)


def iterate(gram_ref, start_ref, basis_ref, rows_ref, product_ref, m_ref, v_ref):
    rows_ref[...] = start_ref[...].T

    def step(_, carry):
        product_ref[...] = contract(rows_ref[...], gram_ref[...], 1, 0)
        m_ref[...] = contract(product_ref[...], product_ref[...], 1, 1)
        inverse_cholesky(m_ref, v_ref)
        rows_ref[...] = contract(v_ref[...], product_ref[...], 1, 0)
        return carry

    lax.fori_loop(0, ITERS, step, 0)
    basis_ref[...] = rows_ref[...].T


def subspace(gram, start):
    columns, rank = start.shape
    return pl.pallas_call(
        iterate,
        out_shape=jax.ShapeDtypeStruct((columns, rank), jnp.float32),
        in_specs=[pl.BlockSpec(memory_space=pltpu.VMEM)] * 2,
        out_specs=pl.BlockSpec(memory_space=pltpu.VMEM),
        scratch_shapes=[
            pltpu.VMEM((rank, columns), jnp.float32),
            pltpu.VMEM((rank, columns), jnp.float32),
            pltpu.VMEM((rank, rank), jnp.float32),
            pltpu.VMEM((rank, rank), jnp.float32),
        ],
        name="subspace",
    )(gram, start)


def on_device(slab, start):
    highest = lax.Precision.HIGHEST
    a_local, points, columns = slab.shape
    matrix = slab.reshape(a_local * points, columns)
    scale = jnp.float32(1.0 / (a_local * points * lax.axis_size("grp") * lax.axis_size(DEV)))
    local_gram = jnp.dot(matrix.T, matrix, precision=highest) * scale
    gram = total_of(local_gram, (("grp", "dev_0", "dev_1"), "dev_2"))
    basis = subspace(gram, start)
    projected = jnp.einsum("abk,kr->bar", slab, basis, precision=highest)
    regrouped = lax.all_to_all(projected, DEV, split_axis=0, concat_axis=1, tiled=True)
    return (regrouped, basis)


def solution(mesh):
    torus = Mesh(
        mesh.devices.reshape(mesh.shape["grp"], 4, 4, 2), ("grp", "dev_0", "dev_1", "dev_2")
    )
    return jax.shard_map(
        on_device,
        mesh=torus,
        in_specs=(P(GRP_DEV, None, None), P()),
        out_specs=(P(DEV, "grp", None), P()),
        check_vma=False,
    )
```

```python
import functools

import jax
import jax.numpy as jnp
from jax import lax
from jax.experimental import pallas as pl
from jax.experimental.pallas import tpu as pltpu
from jax.sharding import Mesh
from jax.sharding import PartitionSpec as P

ITERS = 4
DEV = ("dev_0", "dev_1", "dev_2")
GRP_DEV = ("grp", "dev_0", "dev_1", "dev_2")
AXES = GRP_DEV


HIGHEST = lax.Precision.HIGHEST
BLOCK = 64


def contract(a, b, dim_a, dim_b):
    return lax.dot_general(
        a, b, (((dim_a,), (dim_b,)), ((), ())), precision=HIGHEST, preferred_element_type=jnp.float32
    )


def inverse_factor(block):
    size = block.shape[0]
    diagonal = lax.broadcasted_iota(jnp.int32, (size, size), 0) == lax.broadcasted_iota(jnp.int32, (size, size), 1)
    both = jnp.concatenate([block, diagonal.astype(jnp.float32)], axis=1)
    wide = (8, 2 * size)
    count = size // 8
    tiles = [both[8 * t : 8 * t + 8, :] for t in range(count)]
    row_of = lax.broadcasted_iota(jnp.int32, wide, 0)
    for t in range(count):
        cols = [[jnp.broadcast_to(tiles[u][:, 8 * t + c : 8 * t + c + 1], wide) for u in range(t, count)] for c in range(8)]
        rows = [jnp.broadcast_to(tiles[t][i : i + 1, :], wide) for i in range(8)]
        a = [
            [
                jnp.broadcast_to(jnp.sum(jnp.where(row_of == i, cols[c][0], 0.0), axis=0, keepdims=True), wide)
                if i >= c
                else None
                for c in range(8)
            ]
            for i in range(8)
        ]
        unit = [[None] * 8 for _ in range(8)]
        scaled = []
        for c in range(8):
            inverse = 1.0 / a[c][c]
            for i in range(c + 1, 8):
                unit[i][c] = a[i][c] * inverse
            for k in range(c + 1, 8):
                for i in range(k, 8):
                    a[i][k] = a[i][k] - unit[i][c] * a[k][c]
            for i in range(c + 1, 8):
                rows[i] = rows[i] - unit[i][c] * rows[c]
            scaled.append(rows[c] * inverse)
        for u in range(t + 1, count):
            col = [cols[c][u - t] for c in range(8)]
            for c in range(8):
                for k in range(c + 1, 8):
                    col[k] = col[k] - unit[k][c] * col[c]
            change = col[0] * scaled[0]
            for c in range(1, 8):
                change = change + col[c] * scaled[c]
            tiles[u] = tiles[u] - change
        for c in range(8):
            tiles[t] = jnp.where(row_of == c, rows[c] * lax.rsqrt(a[c][c]), tiles[t])
    return jnp.concatenate(tiles, axis=0)[:, size:]


def inverse_cholesky(m_ref, v_ref):
    size = m_ref.shape[0]
    v_ref[...] = jnp.zeros_like(v_ref)
    for lo in range(0, size, BLOCK):
        hi = lo + BLOCK
        inner = inverse_factor(m_ref[lo:hi, lo:hi])
        if lo:
            v_ref[lo:hi, :lo] = contract(inner, v_ref[lo:hi, :lo], 1, 0)
        v_ref[lo:hi, lo:hi] = inner
        if hi < size:
            across = contract(inner, m_ref[lo:hi, hi:], 1, 0)
            down = contract(m_ref[hi:, lo:hi], inner, 1, 1)
            m_ref[hi:, hi:] -= contract(down, across, 1, 0)
            v_ref[hi:, :hi] -= contract(down, v_ref[lo:hi, :hi], 1, 0)


def iterate(gram_ref, start_ref, basis_ref, rows_ref, product_ref, m_ref, v_ref):
    rows_ref[...] = start_ref[...].T

    def step(_, carry):
        product_ref[...] = contract(rows_ref[...], gram_ref[...], 1, 0)
        m_ref[...] = contract(product_ref[...], product_ref[...], 1, 1)
        inverse_cholesky(m_ref, v_ref)
        rows_ref[...] = contract(v_ref[...], product_ref[...], 1, 0)
        return carry

    lax.fori_loop(0, ITERS, step, 0)
    basis_ref[...] = rows_ref[...].T


def subspace(gram, start):
    columns, rank = start.shape
    return pl.pallas_call(
        iterate,
        out_shape=jax.ShapeDtypeStruct((columns, rank), jnp.float32),
        in_specs=[pl.BlockSpec(memory_space=pltpu.VMEM)] * 2,
        out_specs=pl.BlockSpec(memory_space=pltpu.VMEM),
        scratch_shapes=[
            pltpu.VMEM((rank, columns), jnp.float32),
            pltpu.VMEM((rank, columns), jnp.float32),
            pltpu.VMEM((rank, rank), jnp.float32),
            pltpu.VMEM((rank, rank), jnp.float32),
        ],
        name="subspace",
    )(gram, start)


MESH = pl.DeviceIdType.MESH
TILE = 128
CHUNKS = 4


def halves_of(x):
    high = x.astype(jnp.bfloat16)
    return high, (x - high.astype(jnp.float32)).astype(jnp.bfloat16)


def sum_gram(side, scale, slab_ref, gram_ref, slab, acc, part, pair, mine, arrived, line, whole, load_sem, send_sem, recv_sem):
    y, x, z, core = (lax.axis_index(name) for name in AXES)
    columns = gram_ref.shape[0]
    tiles = columns // TILE
    blocks = [(i, j) for i in range(tiles) for j in range(i, tiles)]
    half = len(blocks) // 2
    place = x * side + z
    plane = [(dx, dz) for dx in range(side) for dz in range(side) if dx or dz]

    def at(dy, dx, dz, dc):
        return {
            "grp": lax.rem(y + dy, side),
            "dev_0": lax.rem(x + dx, side),
            "dev_1": lax.rem(z + dz, side),
            "dev_2": lax.rem(core + dc, 2),
        }

    depth = slab_ref.shape[0] // CHUNKS
    loads = [
        pltpu.make_async_copy(slab_ref.at[pl.ds(n * depth, depth)], slab.at[n], load_sem.at[n]) for n in range(CHUNKS)
    ]
    for load in loads:
        load.start()
    barrier = pltpu.get_barrier_semaphore()
    others = [(0, dx, dz, dc) for dx in range(side) for dz in range(side) for dc in range(2) if dx or dz or dc]
    others += [(dy, 0, 0, 0) for dy in range(1, side)]
    for offsets in others:
        pl.semaphore_signal(barrier, inc=1, device_id=at(*offsets), device_id_type=MESH)

    for n in range(CHUNKS):
        loads[n].wait()
        high, low = halves_of(slab[n].reshape(-1, columns))
        left = jnp.concatenate([high, high, low], axis=0)
        right = jnp.concatenate([high, low, high], axis=0)
        for lo in range(0, columns, 256):
            new = lax.dot_general(
                left[:, : lo + 256], right[:, lo : lo + 256], (((0,), (0,)), ((), ())), preferred_element_type=jnp.float32
            )
            if n:
                new = acc[: lo + 256, lo : lo + 256] + new
            acc[: lo + 256, lo : lo + 256] = new
    for n, (i, j) in enumerate(blocks):
        part[n] = acc[i * TILE : (i + 1) * TILE, j * TILE : (j + 1) * TILE] * scale
    pl.semaphore_wait(barrier, len(others))

    def send(src, dst, slot, offsets):
        return pltpu.make_async_remote_copy(
            src_ref=src,
            dst_ref=dst,
            send_sem=send_sem.at[slot],
            recv_sem=recv_sem.at[slot],
            device_id=at(*offsets),
            device_id_type=MESH,
        )

    swap = send(part.at[pl.ds((1 - core) * half, half)], pair, 0, (0, 0, 0, 1))
    swap.start()
    swap.wait()
    mine[...] = part[pl.ds(core * half, half)] + pair[...]

    def rows_of(index):
        return pl.ds(pl.multiple_of(index * 8, 8), 8)

    copies = []
    for n, (dx, dz) in enumerate(plane):
        target = lax.rem(x + dx, side) * side + lax.rem(z + dz, side)
        copies.append(send(mine.at[:, rows_of(target), :], arrived.at[n], 1 + n, (0, dx, dz, 0)))
        copies[-1].start()
    total = mine[:, rows_of(place), :]
    for n, copy in enumerate(copies):
        copy.wait_recv()
        total = total + arrived[n]
    line[y] = total
    for copy in copies:
        copy.wait_send()

    base = 1 + len(plane)
    copies = []
    for dy in range(1, side):
        copies.append(send(line.at[y], line.at[y], base + dy - 1, (dy, 0, 0, 0)))
        copies[-1].start()
    for copy in copies:
        copy.wait()
    total = line[0]
    for k in range(1, side):
        total = total + line[k]
    own = whole.at[pl.ds(core * half, half), rows_of(place), :]
    own[...] = total

    base += side - 1
    copies = []
    for n, offsets in enumerate(others[: 2 * side * side - 1]):
        copies.append(send(own, own, base + n, offsets))
        copies[-1].start()
    for copy in copies:
        copy.wait()
    for n, (i, j) in enumerate(blocks):
        block = whole[n]
        gram_ref[i * TILE : (i + 1) * TILE, j * TILE : (j + 1) * TILE] = block
        if i != j:
            gram_ref[j * TILE : (j + 1) * TILE, i * TILE : (i + 1) * TILE] = block.T


def summed_gram(slab, scale):
    columns = slab.shape[-1]
    side = lax.axis_size("grp")
    tiles = columns // TILE
    half = tiles * (tiles + 1) // 4
    slots = 3 * side * side + side - 2
    return pl.pallas_call(
        functools.partial(sum_gram, side, scale),
        out_shape=jax.ShapeDtypeStruct((columns, columns), jnp.float32),
        in_specs=[pl.BlockSpec(memory_space=pl.ANY)],
        out_specs=pl.BlockSpec(memory_space=pltpu.VMEM),
        scratch_shapes=[
            pltpu.VMEM((CHUNKS, slab.shape[0] // CHUNKS, *slab.shape[1:]), jnp.float32),
            pltpu.VMEM((columns, columns), jnp.float32),
            pltpu.VMEM((2 * half, TILE, TILE), jnp.float32),
            pltpu.VMEM((half, TILE, TILE), jnp.float32),
            pltpu.VMEM((half, TILE, TILE), jnp.float32),
            pltpu.VMEM((side * side - 1, half, 8, TILE), jnp.float32),
            pltpu.VMEM((side, half, 8, TILE), jnp.float32),
            pltpu.VMEM((2 * half, TILE, TILE), jnp.float32),
            pltpu.SemaphoreType.DMA((CHUNKS,)),
            pltpu.SemaphoreType.DMA((slots,)),
            pltpu.SemaphoreType.DMA((slots,)),
        ],
        compiler_params=pltpu.CompilerParams(collective_id=0, has_side_effects=True),
        name="sum_gram",
    )(slab)


def on_device(slab, start):
    highest = lax.Precision.HIGHEST
    a_local, points, columns = slab.shape
    scale = 1.0 / (a_local * points * lax.axis_size("grp") * lax.axis_size(DEV))
    gram = summed_gram(slab, scale)
    basis = subspace(gram, start)
    projected = jnp.einsum("abk,kr->bar", slab, basis, precision=highest)
    regrouped = lax.all_to_all(projected, DEV, split_axis=0, concat_axis=1, tiled=True)
    return (regrouped, basis)


def solution(mesh):
    torus = Mesh(
        mesh.devices.reshape(mesh.shape["grp"], 4, 4, 2), ("grp", "dev_0", "dev_1", "dev_2")
    )
    return jax.shard_map(
        on_device,
        mesh=torus,
        in_specs=(P(GRP_DEV, None, None), P()),
        out_specs=(P(DEV, "grp", None), P()),
        check_vma=False,
    )
```

```python
import functools

import jax
import jax.numpy as jnp
from jax import lax
from jax.experimental import pallas as pl
from jax.experimental.pallas import tpu as pltpu
from jax.sharding import Mesh
from jax.sharding import PartitionSpec as P

ITERS = 4
DEV = ("dev_0", "dev_1", "dev_2")
GRP_DEV = ("grp", "dev_0", "dev_1", "dev_2")
AXES = GRP_DEV
MESH = pl.DeviceIdType.MESH


HIGHEST = lax.Precision.HIGHEST
BLOCK = 64


def contract(a, b, dim_a, dim_b):
    return lax.dot_general(
        a, b, (((dim_a,), (dim_b,)), ((), ())), precision=HIGHEST, preferred_element_type=jnp.float32
    )


def inverse_factor(block):
    size = block.shape[0]
    diagonal = lax.broadcasted_iota(jnp.int32, (size, size), 0) == lax.broadcasted_iota(jnp.int32, (size, size), 1)
    both = jnp.concatenate([block, diagonal.astype(jnp.float32)], axis=1)
    wide = (8, 2 * size)
    count = size // 8
    tiles = [both[8 * t : 8 * t + 8, :] for t in range(count)]
    row_of = lax.broadcasted_iota(jnp.int32, wide, 0)
    for t in range(count):
        cols = [[jnp.broadcast_to(tiles[u][:, 8 * t + c : 8 * t + c + 1], wide) for u in range(t, count)] for c in range(8)]
        rows = [jnp.broadcast_to(tiles[t][i : i + 1, :], wide) for i in range(8)]
        a = [
            [
                jnp.broadcast_to(jnp.sum(jnp.where(row_of == i, cols[c][0], 0.0), axis=0, keepdims=True), wide)
                if i >= c
                else None
                for c in range(8)
            ]
            for i in range(8)
        ]
        unit = [[None] * 8 for _ in range(8)]
        scaled = []
        for c in range(8):
            inverse = 1.0 / a[c][c]
            for i in range(c + 1, 8):
                unit[i][c] = a[i][c] * inverse
            for k in range(c + 1, 8):
                for i in range(k, 8):
                    a[i][k] = a[i][k] - unit[i][c] * a[k][c]
            for i in range(c + 1, 8):
                rows[i] = rows[i] - unit[i][c] * rows[c]
            scaled.append(rows[c] * inverse)
        for u in range(t + 1, count):
            col = [cols[c][u - t] for c in range(8)]
            for c in range(8):
                for k in range(c + 1, 8):
                    col[k] = col[k] - unit[k][c] * col[c]
            change = col[0] * scaled[0]
            for c in range(1, 8):
                change = change + col[c] * scaled[c]
            tiles[u] = tiles[u] - change
        for c in range(8):
            tiles[t] = jnp.where(row_of == c, rows[c] * lax.rsqrt(a[c][c]), tiles[t])
    return jnp.concatenate(tiles, axis=0)[:, size:]


def inverse_cholesky(m_ref, v_ref):
    size = m_ref.shape[0]
    v_ref[...] = jnp.zeros_like(v_ref)
    for lo in range(0, size, BLOCK):
        hi = lo + BLOCK
        inner = inverse_factor(m_ref[lo:hi, lo:hi])
        if lo:
            v_ref[lo:hi, :lo] = contract(inner, v_ref[lo:hi, :lo], 1, 0)
        v_ref[lo:hi, lo:hi] = inner
        if hi < size:
            across = contract(inner, m_ref[lo:hi, hi:], 1, 0)
            down = contract(m_ref[hi:, lo:hi], inner, 1, 1)
            m_ref[hi:, hi:] -= contract(down, across, 1, 0)
            v_ref[hi:, :hi] -= contract(down, v_ref[lo:hi, :hi], 1, 0)


def iterate(side, gram_ref, start_ref, slab_ref, basis_ref, moved_ref, rows_ref, product_ref, m_ref, v_ref, own_sem, send_sem, recv_sem):
    x, z, core = (lax.axis_index(name) for name in DEV)
    count = slab_ref.shape[0]
    held = moved_ref.shape[0]

    def place(x, z, core):
        return (x * side + z) * 2 + core

    def rows_here(index):
        return pl.ds(pl.multiple_of(index * count, count), count)

    peers = []
    for dx in range(side):
        for dz in range(side):
            for dc in range(2):
                if dx or dz or dc:
                    peers.append((lax.rem(x + dx, side), lax.rem(z + dz, side), lax.rem(core + dc, 2)))
    barrier = pltpu.get_barrier_semaphore()
    for peer in peers:
        pl.semaphore_signal(barrier, inc=1, device_id=dict(zip(DEV, peer)), device_id_type=MESH)
    pl.semaphore_wait(barrier, len(peers))
    me = place(x, z, core)
    copies = []
    for n, peer in enumerate(peers):
        for i in range(held):
            copies.append(
                pltpu.make_async_remote_copy(
                    src_ref=slab_ref.at[:, place(*peer) * held + i, :],
                    dst_ref=moved_ref.at[i, rows_here(me), :],
                    send_sem=send_sem.at[n, i],
                    recv_sem=recv_sem.at[n, i],
                    device_id=dict(zip(DEV, peer)),
                    device_id_type=MESH,
                )
            )
    for i in range(held):
        copies.append(
            pltpu.make_async_copy(slab_ref.at[:, me * held + i, :], moved_ref.at[i, rows_here(me), :], own_sem.at[i])
        )
    for copy in copies:
        copy.start()

    rows_ref[...] = start_ref[...].T

    def step(_, carry):
        product_ref[...] = contract(rows_ref[...], gram_ref[...], 1, 0)
        m_ref[...] = contract(product_ref[...], product_ref[...], 1, 1)
        inverse_cholesky(m_ref, v_ref)
        rows_ref[...] = contract(v_ref[...], product_ref[...], 1, 0)
        return carry

    lax.fori_loop(0, ITERS, step, 0)
    basis_ref[...] = rows_ref[...].T
    for copy in copies:
        copy.wait()


def subspace(gram, start, slab):
    columns, rank = start.shape
    count, points, _ = slab.shape
    peers = lax.axis_size(DEV)
    held = points // peers
    vmem = pl.BlockSpec(memory_space=pltpu.VMEM)
    hbm = pl.BlockSpec(memory_space=pl.ANY)
    return pl.pallas_call(
        functools.partial(iterate, lax.axis_size("grp")),
        out_shape=(
            jax.ShapeDtypeStruct((columns, rank), jnp.float32),
            jax.ShapeDtypeStruct((held, count * peers, columns), jnp.float32),
        ),
        in_specs=[vmem, vmem, hbm],
        out_specs=(vmem, hbm),
        scratch_shapes=[
            pltpu.VMEM((rank, columns), jnp.float32),
            pltpu.VMEM((rank, columns), jnp.float32),
            pltpu.VMEM((rank, rank), jnp.float32),
            pltpu.VMEM((rank, rank), jnp.float32),
            pltpu.SemaphoreType.DMA((held,)),
            pltpu.SemaphoreType.DMA((peers - 1, held)),
            pltpu.SemaphoreType.DMA((peers - 1, held)),
        ],
        compiler_params=pltpu.CompilerParams(collective_id=1, has_side_effects=True),
        name="subspace",
    )(gram, start, slab)


def project(rows_ref, basis_ref, out_ref):
    high, low = halves_of(rows_ref[...])
    basis_high, basis_low = halves_of(basis_ref[...])
    left = jnp.concatenate([high, high, low], axis=1)
    right = jnp.concatenate([basis_high, basis_low, basis_high], axis=0)
    out_ref[...] = lax.dot_general(left, right, (((1,), (0,)), ((), ())), preferred_element_type=jnp.float32)


def projected_rows(moved, basis):
    held, count, columns = moved.shape
    rank = basis.shape[1]
    rows = 256
    return pl.pallas_call(
        project,
        out_shape=jax.ShapeDtypeStruct((held * count, rank), jnp.float32),
        grid=(held * count // rows,),
        in_specs=[
            pl.BlockSpec((rows, columns), lambda n: (n, 0)),
            pl.BlockSpec((columns, rank), lambda n: (0, 0)),
        ],
        out_specs=pl.BlockSpec((rows, rank), lambda n: (n, 0)),
        name="project",
    )(moved.reshape(held * count, columns), basis).reshape(held, count, rank)


TILE = 128
CHUNKS = 4


def halves_of(x):
    high = x.astype(jnp.bfloat16)
    return high, (x - high.astype(jnp.float32)).astype(jnp.bfloat16)


def sum_gram(side, scale, slab_ref, gram_ref, slab, acc, part, pair, mine, arrived, line, whole, load_sem, send_sem, recv_sem):
    y, x, z, core = (lax.axis_index(name) for name in AXES)
    columns = gram_ref.shape[0]
    tiles = columns // TILE
    blocks = [(i, j) for i in range(tiles) for j in range(i, tiles)]
    half = len(blocks) // 2
    place = x * side + z
    plane = [(dx, dz) for dx in range(side) for dz in range(side) if dx or dz]

    def at(dy, dx, dz, dc):
        return {
            "grp": lax.rem(y + dy, side),
            "dev_0": lax.rem(x + dx, side),
            "dev_1": lax.rem(z + dz, side),
            "dev_2": lax.rem(core + dc, 2),
        }

    depth = slab_ref.shape[0] // CHUNKS
    loads = [
        pltpu.make_async_copy(slab_ref.at[pl.ds(n * depth, depth)], slab.at[n], load_sem.at[n]) for n in range(CHUNKS)
    ]
    for load in loads:
        load.start()
    barrier = pltpu.get_barrier_semaphore()
    others = [(0, dx, dz, dc) for dx in range(side) for dz in range(side) for dc in range(2) if dx or dz or dc]
    others += [(dy, 0, 0, 0) for dy in range(1, side)]
    for offsets in others:
        pl.semaphore_signal(barrier, inc=1, device_id=at(*offsets), device_id_type=MESH)

    for n in range(CHUNKS):
        loads[n].wait()
        high, low = halves_of(slab[n].reshape(-1, columns))
        left = jnp.concatenate([high, high, low], axis=0)
        right = jnp.concatenate([high, low, high], axis=0)
        for lo in range(0, columns, 256):
            new = lax.dot_general(
                left[:, : lo + 256], right[:, lo : lo + 256], (((0,), (0,)), ((), ())), preferred_element_type=jnp.float32
            )
            if n:
                new = acc[: lo + 256, lo : lo + 256] + new
            acc[: lo + 256, lo : lo + 256] = new
    for n, (i, j) in enumerate(blocks):
        part[n] = acc[i * TILE : (i + 1) * TILE, j * TILE : (j + 1) * TILE] * scale
    pl.semaphore_wait(barrier, len(others))

    def send(src, dst, slot, offsets):
        return pltpu.make_async_remote_copy(
            src_ref=src,
            dst_ref=dst,
            send_sem=send_sem.at[slot],
            recv_sem=recv_sem.at[slot],
            device_id=at(*offsets),
            device_id_type=MESH,
        )

    swap = send(part.at[pl.ds((1 - core) * half, half)], pair, 0, (0, 0, 0, 1))
    swap.start()
    swap.wait()
    mine[...] = part[pl.ds(core * half, half)] + pair[...]

    def rows_of(index):
        return pl.ds(pl.multiple_of(index * 8, 8), 8)

    copies = []
    for n, (dx, dz) in enumerate(plane):
        target = lax.rem(x + dx, side) * side + lax.rem(z + dz, side)
        copies.append(send(mine.at[:, rows_of(target), :], arrived.at[n], 1 + n, (0, dx, dz, 0)))
        copies[-1].start()
    total = mine[:, rows_of(place), :]
    for n, copy in enumerate(copies):
        copy.wait_recv()
        total = total + arrived[n]
    line[y] = total
    for copy in copies:
        copy.wait_send()

    base = 1 + len(plane)
    copies = []
    for dy in range(1, side):
        copies.append(send(line.at[y], line.at[y], base + dy - 1, (dy, 0, 0, 0)))
        copies[-1].start()
    for copy in copies:
        copy.wait()
    total = line[0]
    for k in range(1, side):
        total = total + line[k]
    own = whole.at[pl.ds(core * half, half), rows_of(place), :]
    own[...] = total

    base += side - 1
    copies = []
    for n, offsets in enumerate(others[: 2 * side * side - 1]):
        copies.append(send(own, own, base + n, offsets))
        copies[-1].start()
    for copy in copies:
        copy.wait()
    for n, (i, j) in enumerate(blocks):
        block = whole[n]
        gram_ref[i * TILE : (i + 1) * TILE, j * TILE : (j + 1) * TILE] = block
        if i != j:
            gram_ref[j * TILE : (j + 1) * TILE, i * TILE : (i + 1) * TILE] = block.T


def summed_gram(slab, scale):
    columns = slab.shape[-1]
    side = lax.axis_size("grp")
    tiles = columns // TILE
    half = tiles * (tiles + 1) // 4
    slots = 3 * side * side + side - 2
    return pl.pallas_call(
        functools.partial(sum_gram, side, scale),
        out_shape=jax.ShapeDtypeStruct((columns, columns), jnp.float32),
        in_specs=[pl.BlockSpec(memory_space=pl.ANY)],
        out_specs=pl.BlockSpec(memory_space=pltpu.VMEM),
        scratch_shapes=[
            pltpu.VMEM((CHUNKS, slab.shape[0] // CHUNKS, *slab.shape[1:]), jnp.float32),
            pltpu.VMEM((columns, columns), jnp.float32),
            pltpu.VMEM((2 * half, TILE, TILE), jnp.float32),
            pltpu.VMEM((half, TILE, TILE), jnp.float32),
            pltpu.VMEM((half, TILE, TILE), jnp.float32),
            pltpu.VMEM((side * side - 1, half, 8, TILE), jnp.float32),
            pltpu.VMEM((side, half, 8, TILE), jnp.float32),
            pltpu.VMEM((2 * half, TILE, TILE), jnp.float32),
            pltpu.SemaphoreType.DMA((CHUNKS,)),
            pltpu.SemaphoreType.DMA((slots,)),
            pltpu.SemaphoreType.DMA((slots,)),
        ],
        compiler_params=pltpu.CompilerParams(collective_id=0, has_side_effects=True),
        name="sum_gram",
    )(slab)


def on_device(slab, start):
    a_local, points, _ = slab.shape
    scale = 1.0 / (a_local * points * lax.axis_size("grp") * lax.axis_size(DEV))
    gram = summed_gram(slab, scale)
    basis, moved = subspace(gram, start, slab)
    return (projected_rows(moved, basis), basis)


def solution(mesh):
    torus = Mesh(
        mesh.devices.reshape(mesh.shape["grp"], 4, 4, 2), ("grp", "dev_0", "dev_1", "dev_2")
    )
    return jax.shard_map(
        on_device,
        mesh=torus,
        in_specs=(P(GRP_DEV, None, None), P()),
        out_specs=(P(DEV, "grp", None), P()),
        check_vma=False,
    )
```

```python
import functools

import jax
import jax.numpy as jnp
from jax import lax
from jax.experimental import pallas as pl
from jax.experimental.pallas import tpu as pltpu
from jax.sharding import Mesh
from jax.sharding import PartitionSpec as P

ITERS = 4
DEV = ("dev_0", "dev_1", "dev_2")
GRP_DEV = ("grp", "dev_0", "dev_1", "dev_2")
AXES = GRP_DEV
MESH = pl.DeviceIdType.MESH


HIGHEST = lax.Precision.HIGHEST
BLOCK = 64
PANEL = 16


def contract(a, b, dim_a, dim_b):
    return lax.dot_general(
        a, b, (((dim_a,), (dim_b,)), ((), ())), precision=HIGHEST, preferred_element_type=jnp.float32
    )


def inverse_factor(block, spread_ref):
    size = block.shape[0]
    diagonal = lax.broadcasted_iota(jnp.int32, (size, size), 0) == lax.broadcasted_iota(jnp.int32, (size, size), 1)
    both = jnp.concatenate([block, diagonal.astype(jnp.float32)], axis=1)
    wide = (8, 2 * size)
    count = size // 8
    tiles = [both[8 * t : 8 * t + 8, :] for t in range(count)]
    row_of = lax.broadcasted_iota(jnp.int32, wide, 0)

    def over_rows(row):
        return jnp.broadcast_to(row, wide)

    for first in range(0, count, PANEL // 8):
        after = first + PANEL // 8
        cols = [
            [jnp.broadcast_to(tiles[u][:, 8 * first + c : 8 * first + c + 1], wide) for u in range(first, count)]
            for c in range(PANEL)
        ]
        for t in range(first, after):
            spread_ref[PANEL + t - first] = tiles[t]
        spread_ref[0] = cols[0][0]
        for t in range(1, PANEL // 8):
            spread_ref[PANEL + PANEL // 8 + t - 1] = cols[0][t]
        rows = [over_rows(spread_ref[PANEL + i // 8, i % 8 : i % 8 + 1, :]) for i in range(PANEL)]
        pivots, scaled = [], []
        for c in range(PANEL):
            def at(i):
                if c == 0:
                    slot = 0 if i < 8 else PANEL + PANEL // 8 + i // 8 - 1
                    return over_rows(spread_ref[slot, i % 8 : i % 8 + 1, :])
                return over_rows(cols[c][i // 8][i % 8 : i % 8 + 1, :])

            pivots.append(at(c))
            inverse = 1.0 / pivots[c]
            for k in range(c + 1, PANEL):
                factor = at(k) * inverse
                for u in range(k // 8, count - first):
                    cols[k][u] = cols[k][u] - factor * cols[c][u]
                rows[k] = rows[k] - factor * rows[c]
            scaled.append(rows[c] * inverse)
        for u in range(after, count):
            change = cols[0][u - first] * scaled[0]
            for c in range(1, PANEL):
                change = change + cols[c][u - first] * scaled[c]
            tiles[u] = tiles[u] - change
        for c in range(PANEL):
            t = first + c // 8
            tiles[t] = jnp.where(row_of == c % 8, rows[c] * lax.rsqrt(pivots[c]), tiles[t])
    return jnp.concatenate(tiles, axis=0)[:, size:]


def inverse_cholesky(m_ref, v_ref, spread_ref):
    size = m_ref.shape[0]
    v_ref[...] = jnp.zeros_like(v_ref)
    corner = m_ref[:BLOCK, :BLOCK]
    for lo in range(0, size, BLOCK):
        hi = lo + BLOCK
        end = min(hi + BLOCK, size)
        inner = inverse_factor(corner, spread_ref)
        if hi < size:
            across = contract(inner, m_ref[lo:hi, hi:end], 1, 0)
            down = contract(m_ref[hi:end, lo:hi], inner, 1, 1)
            corner = m_ref[hi:end, hi:end] - contract(down, across, 1, 0)
        if lo:
            v_ref[lo:hi, :lo] = contract(inner, v_ref[lo:hi, :lo], 1, 0)
        v_ref[lo:hi, lo:hi] = inner
        if end < size:
            far_across = contract(inner, m_ref[lo:hi, end:], 1, 0)
            far_down = contract(m_ref[end:, lo:hi], inner, 1, 1)
            m_ref[hi:end, end:] -= contract(down, far_across, 1, 0)
            m_ref[end:, hi:end] -= contract(far_down, across, 1, 0)
            m_ref[end:, end:] -= contract(far_down, far_across, 1, 0)
            v_ref[end:, :hi] -= contract(far_down, v_ref[lo:hi, :hi], 1, 0)
        if hi < size:
            v_ref[hi:end, :hi] -= contract(down, v_ref[lo:hi, :hi], 1, 0)


def far_first(side):
    def hops(offset):
        return sum(min(step, side - step) for step in offset)

    order = []
    for dx, dz in sorted(((dx, dz) for dx in range(side) for dz in range(side)), key=lambda o: (-hops(o), o)):
        back_x, back_z = (side - dx) % side, (side - dz) % side
        for offset in ((dx, dz), (back_x, back_z), (dz, back_x), (back_z, dx)):
            if offset not in order and any(offset):
                order.append(offset)
    return order


def iterate(side, gram_ref, start_ref, slab_ref, basis_ref, moved_ref, rows_ref, product_ref, m_ref, v_ref, spread_ref, own_sem, send_sem, recv_sem):
    x, z, core = (lax.axis_index(name) for name in DEV)
    count = slab_ref.shape[0]
    held = moved_ref.shape[0]

    def place(x, z, core):
        return (x * side + z) * 2 + core

    def rows_here(index):
        return pl.ds(pl.multiple_of(index * count, count), count)

    peers = [(x, z, 1 - core)]
    for dx, dz in far_first(side):
        for dc in range(2):
            step_x = dx + core * ((side - dx) % side - dx)
            step_z = dz + core * ((side - dz) % side - dz)
            peers.append((lax.rem(x + step_x, side), lax.rem(z + step_z, side), lax.rem(core + dc, 2)))
    barrier = pltpu.get_barrier_semaphore()
    for peer in peers:
        pl.semaphore_signal(barrier, inc=1, device_id=dict(zip(DEV, peer)), device_id_type=MESH)
    pl.semaphore_wait(barrier, len(peers))
    me = place(x, z, core)
    copies = []
    for n, peer in enumerate(peers):
        for i in range(held):
            copies.append(
                pltpu.make_async_remote_copy(
                    src_ref=slab_ref.at[:, place(*peer) * held + i, :],
                    dst_ref=moved_ref.at[i, rows_here(me), :],
                    send_sem=send_sem.at[n, i],
                    recv_sem=recv_sem.at[n, i],
                    device_id=dict(zip(DEV, peer)),
                    device_id_type=MESH,
                )
            )
    for i in range(held):
        copies.append(
            pltpu.make_async_copy(slab_ref.at[:, me * held + i, :], moved_ref.at[i, rows_here(me), :], own_sem.at[i])
        )
    for copy in copies:
        copy.start()

    rows_ref[...] = start_ref[...].T

    def step(_, carry):
        product_ref[...] = contract(rows_ref[...], gram_ref[...], 1, 0)
        m_ref[...] = contract(product_ref[...], product_ref[...], 1, 1)
        inverse_cholesky(m_ref, v_ref, spread_ref)
        rows_ref[...] = contract(v_ref[...], product_ref[...], 1, 0)
        return carry

    lax.fori_loop(0, ITERS, step, 0)
    basis_ref[...] = rows_ref[...].T
    for copy in copies:
        copy.wait()


def subspace(gram, start, slab):
    columns, rank = start.shape
    count, points, _ = slab.shape
    peers = lax.axis_size(DEV)
    held = points // peers
    vmem = pl.BlockSpec(memory_space=pltpu.VMEM)
    hbm = pl.BlockSpec(memory_space=pl.ANY)
    return pl.pallas_call(
        functools.partial(iterate, lax.axis_size("grp")),
        out_shape=(
            jax.ShapeDtypeStruct((columns, rank), jnp.float32),
            jax.ShapeDtypeStruct((held, count * peers, columns), jnp.float32),
        ),
        in_specs=[vmem, vmem, hbm],
        out_specs=(vmem, hbm),
        scratch_shapes=[
            pltpu.VMEM((rank, columns), jnp.float32),
            pltpu.VMEM((rank, columns), jnp.float32),
            pltpu.VMEM((rank, rank), jnp.float32),
            pltpu.VMEM((rank, rank), jnp.float32),
            pltpu.VMEM((PANEL + PANEL // 4, 8, 2 * BLOCK), jnp.float32),
            pltpu.SemaphoreType.DMA((held,)),
            pltpu.SemaphoreType.DMA((peers - 1, held)),
            pltpu.SemaphoreType.DMA((peers - 1, held)),
        ],
        compiler_params=pltpu.CompilerParams(collective_id=1, has_side_effects=True),
        name="subspace",
    )(gram, start, slab)


def project(rows_ref, basis_ref, out_ref):
    high, low = halves_of(rows_ref[...])
    basis_high, basis_low = halves_of(basis_ref[...])
    left = jnp.concatenate([high, high, low], axis=1)
    right = jnp.concatenate([basis_high, basis_low, basis_high], axis=0)
    out_ref[...] = lax.dot_general(left, right, (((1,), (0,)), ((), ())), preferred_element_type=jnp.float32)


def projected_rows(moved, basis):
    held, count, columns = moved.shape
    rank = basis.shape[1]
    rows = 256
    return pl.pallas_call(
        project,
        out_shape=jax.ShapeDtypeStruct((held * count, rank), jnp.float32),
        grid=(held * count // rows,),
        in_specs=[
            pl.BlockSpec((rows, columns), lambda n: (n, 0)),
            pl.BlockSpec((columns, rank), lambda n: (0, 0)),
        ],
        out_specs=pl.BlockSpec((rows, rank), lambda n: (n, 0)),
        name="project",
    )(moved.reshape(held * count, columns), basis).reshape(held, count, rank)


TILE = 128
CHUNKS = 4


def halves_of(x):
    high = x.astype(jnp.bfloat16)
    return high, (x - high.astype(jnp.float32)).astype(jnp.bfloat16)


def sum_gram(side, scale, slab_ref, gram_ref, slab, acc, part, pair, mine, arrived, line, whole, load_sem, send_sem, recv_sem):
    y, x, z, core = (lax.axis_index(name) for name in AXES)
    columns = gram_ref.shape[0]
    tiles = columns // TILE
    blocks = [(i, j) for i in range(tiles) for j in range(i, tiles)]
    half = len(blocks) // 2
    place = x * side + z
    plane = [(dx, dz) for dx in range(side) for dz in range(side) if dx or dz]

    def at(dy, dx, dz, dc):
        return {
            "grp": lax.rem(y + dy, side),
            "dev_0": lax.rem(x + dx, side),
            "dev_1": lax.rem(z + dz, side),
            "dev_2": lax.rem(core + dc, 2),
        }

    depth = slab_ref.shape[0] // CHUNKS
    loads = [
        pltpu.make_async_copy(slab_ref.at[pl.ds(n * depth, depth)], slab.at[n], load_sem.at[n]) for n in range(CHUNKS)
    ]
    for load in loads:
        load.start()
    barrier = pltpu.get_barrier_semaphore()
    others = [(0, dx, dz, dc) for dx in range(side) for dz in range(side) for dc in range(2) if dx or dz or dc]
    others += [(dy, 0, 0, 0) for dy in range(1, side)]
    for offsets in others:
        pl.semaphore_signal(barrier, inc=1, device_id=at(*offsets), device_id_type=MESH)

    for n in range(CHUNKS):
        loads[n].wait()
        high, low = halves_of(slab[n].reshape(-1, columns))
        left = jnp.concatenate([high, high, low], axis=0)
        right = jnp.concatenate([high, low, high], axis=0)
        for lo in range(0, columns, 256):
            new = lax.dot_general(
                left[:, : lo + 256], right[:, lo : lo + 256], (((0,), (0,)), ((), ())), preferred_element_type=jnp.float32
            )
            if n:
                new = acc[: lo + 256, lo : lo + 256] + new
            acc[: lo + 256, lo : lo + 256] = new
    for n, (i, j) in enumerate(blocks):
        part[n] = acc[i * TILE : (i + 1) * TILE, j * TILE : (j + 1) * TILE] * scale
    pl.semaphore_wait(barrier, len(others))

    def send(src, dst, slot, offsets):
        return pltpu.make_async_remote_copy(
            src_ref=src,
            dst_ref=dst,
            send_sem=send_sem.at[slot],
            recv_sem=recv_sem.at[slot],
            device_id=at(*offsets),
            device_id_type=MESH,
        )

    swap = send(part.at[pl.ds((1 - core) * half, half)], pair, 0, (0, 0, 0, 1))
    swap.start()
    swap.wait()
    mine[...] = part[pl.ds(core * half, half)] + pair[...]

    def rows_of(index):
        return pl.ds(pl.multiple_of(index * 8, 8), 8)

    copies = []
    for n, (dx, dz) in enumerate(plane):
        target = lax.rem(x + dx, side) * side + lax.rem(z + dz, side)
        copies.append(send(mine.at[:, rows_of(target), :], arrived.at[n], 1 + n, (0, dx, dz, 0)))
        copies[-1].start()
    total = mine[:, rows_of(place), :]
    for n, copy in enumerate(copies):
        copy.wait_recv()
        total = total + arrived[n]
    line[y] = total
    for copy in copies:
        copy.wait_send()

    base = 1 + len(plane)
    copies = []
    for dy in range(1, side):
        copies.append(send(line.at[y], line.at[y], base + dy - 1, (dy, 0, 0, 0)))
        copies[-1].start()
    for copy in copies:
        copy.wait()
    total = line[0]
    for k in range(1, side):
        total = total + line[k]
    own = whole.at[pl.ds(core * half, half), rows_of(place), :]
    own[...] = total

    base += side - 1
    copies = []
    for n, offsets in enumerate(others[: 2 * side * side - 1]):
        copies.append(send(own, own, base + n, offsets))
        copies[-1].start()
    for copy in copies:
        copy.wait()
    for n, (i, j) in enumerate(blocks):
        block = whole[n]
        gram_ref[i * TILE : (i + 1) * TILE, j * TILE : (j + 1) * TILE] = block
        if i != j:
            gram_ref[j * TILE : (j + 1) * TILE, i * TILE : (i + 1) * TILE] = block.T


def summed_gram(slab, scale):
    columns = slab.shape[-1]
    side = lax.axis_size("grp")
    tiles = columns // TILE
    half = tiles * (tiles + 1) // 4
    slots = 3 * side * side + side - 2
    return pl.pallas_call(
        functools.partial(sum_gram, side, scale),
        out_shape=jax.ShapeDtypeStruct((columns, columns), jnp.float32),
        in_specs=[pl.BlockSpec(memory_space=pl.ANY)],
        out_specs=pl.BlockSpec(memory_space=pltpu.VMEM),
        scratch_shapes=[
            pltpu.VMEM((CHUNKS, slab.shape[0] // CHUNKS, *slab.shape[1:]), jnp.float32),
            pltpu.VMEM((columns, columns), jnp.float32),
            pltpu.VMEM((2 * half, TILE, TILE), jnp.float32),
            pltpu.VMEM((half, TILE, TILE), jnp.float32),
            pltpu.VMEM((half, TILE, TILE), jnp.float32),
            pltpu.VMEM((side * side - 1, half, 8, TILE), jnp.float32),
            pltpu.VMEM((side, half, 8, TILE), jnp.float32),
            pltpu.VMEM((2 * half, TILE, TILE), jnp.float32),
            pltpu.SemaphoreType.DMA((CHUNKS,)),
            pltpu.SemaphoreType.DMA((slots,)),
            pltpu.SemaphoreType.DMA((slots,)),
        ],
        compiler_params=pltpu.CompilerParams(collective_id=0, has_side_effects=True),
        name="sum_gram",
    )(slab)


def on_device(slab, start):
    a_local, points, _ = slab.shape
    scale = 1.0 / (a_local * points * lax.axis_size("grp") * lax.axis_size(DEV))
    gram = summed_gram(slab, scale)
    basis, moved = subspace(gram, start, slab)
    return (projected_rows(moved, basis), basis)


def solution(mesh):
    torus = Mesh(
        mesh.devices.reshape(mesh.shape["grp"], 4, 4, 2), ("grp", "dev_0", "dev_1", "dev_2")
    )
    return jax.shard_map(
        on_device,
        mesh=torus,
        in_specs=(P(GRP_DEV, None, None), P()),
        out_specs=(P(DEV, "grp", None), P()),
        check_vma=False,
    )
```

```python
import functools

import jax
import jax.numpy as jnp
from jax import lax
from jax.experimental import pallas as pl
from jax.experimental.pallas import tpu as pltpu
from jax.sharding import Mesh
from jax.sharding import PartitionSpec as P

ITERS = 4
DEV = ("dev_0", "dev_1", "dev_2")
AXES = ("grp", *DEV)
MESH = pl.DeviceIdType.MESH
HIGHEST = lax.Precision.HIGHEST
BLOCK = 64
PANEL = 16
TILE = 128
CHUNKS = 4
STRIPE = 256
EARLY = 9
MIDDLE = 2


def contract(a, b, dim_a, dim_b):
    return lax.dot_general(
        a, b, (((dim_a,), (dim_b,)), ((), ())), precision=HIGHEST, preferred_element_type=jnp.float32
    )


def inverse_factor(block, spread_ref):
    size = block.shape[0]
    diagonal = lax.broadcasted_iota(jnp.int32, (size, size), 0) == lax.broadcasted_iota(jnp.int32, (size, size), 1)
    both = jnp.concatenate([block, diagonal.astype(jnp.float32)], axis=1)
    wide = (8, 2 * size)
    count = size // 8
    tiles = [both[8 * t : 8 * t + 8, :] for t in range(count)]
    row_of = lax.broadcasted_iota(jnp.int32, wide, 0)

    def over_rows(row):
        return jnp.broadcast_to(row, wide)

    for first in range(0, count, PANEL // 8):
        after = first + PANEL // 8
        cols = [
            [jnp.broadcast_to(tiles[u][:, 8 * first + c : 8 * first + c + 1], wide) for u in range(first, count)]
            for c in range(PANEL)
        ]
        for t in range(first, after):
            spread_ref[PANEL + t - first] = tiles[t]
        spread_ref[0] = cols[0][0]
        for t in range(1, PANEL // 8):
            spread_ref[PANEL + PANEL // 8 + t - 1] = cols[0][t]
        rows = [over_rows(spread_ref[PANEL + i // 8, i % 8 : i % 8 + 1, :]) for i in range(PANEL)]
        pivots, scaled = [], []
        for c in range(PANEL):
            def at(i):
                if c == 0:
                    slot = 0 if i < 8 else PANEL + PANEL // 8 + i // 8 - 1
                    return over_rows(spread_ref[slot, i % 8 : i % 8 + 1, :])
                return over_rows(cols[c][i // 8][i % 8 : i % 8 + 1, :])

            pivots.append(at(c))
            inverse = 1.0 / pivots[c]
            for k in range(c + 1, PANEL):
                factor = at(k) * inverse
                for u in range(k // 8, count - first):
                    cols[k][u] = cols[k][u] - factor * cols[c][u]
                rows[k] = rows[k] - factor * rows[c]
            scaled.append(rows[c] * inverse)
        for u in range(after, count):
            change = cols[0][u - first] * scaled[0]
            for c in range(1, PANEL):
                change = change + cols[c][u - first] * scaled[c]
            tiles[u] = tiles[u] - change
        for c in range(PANEL):
            t = first + c // 8
            tiles[t] = jnp.where(row_of == c % 8, rows[c] * lax.rsqrt(pivots[c]), tiles[t])
    return jnp.concatenate(tiles, axis=0)[:, size:]


def inverse_cholesky(m_ref, v_ref, spread_ref):
    size = m_ref.shape[0]
    v_ref[...] = jnp.zeros_like(v_ref)
    corner = m_ref[:BLOCK, :BLOCK]
    for lo in range(0, size, BLOCK):
        hi = lo + BLOCK
        end = min(hi + BLOCK, size)
        inner = inverse_factor(corner, spread_ref)
        if hi < size:
            across = contract(inner, m_ref[lo:hi, hi:end], 1, 0)
            down = contract(m_ref[hi:end, lo:hi], inner, 1, 1)
            corner = m_ref[hi:end, hi:end] - contract(down, across, 1, 0)
        if lo:
            v_ref[lo:hi, :lo] = contract(inner, v_ref[lo:hi, :lo], 1, 0)
        v_ref[lo:hi, lo:hi] = inner
        if end < size:
            far_across = contract(inner, m_ref[lo:hi, end:], 1, 0)
            far_down = contract(m_ref[end:, lo:hi], inner, 1, 1)
            m_ref[hi:end, end:] -= contract(down, far_across, 1, 0)
            m_ref[end:, hi:end] -= contract(far_down, across, 1, 0)
            m_ref[end:, end:] -= contract(far_down, far_across, 1, 0)
            v_ref[end:, :hi] -= contract(far_down, v_ref[lo:hi, :hi], 1, 0)
        if hi < size:
            v_ref[hi:end, :hi] -= contract(down, v_ref[lo:hi, :hi], 1, 0)


def far_first(side):
    def hops(offset):
        return sum(min(step, side - step) for step in offset)

    order = []
    for dx, dz in sorted(((dx, dz) for dx in range(side) for dz in range(side)), key=lambda o: (-hops(o), o)):
        back_x, back_z = (side - dx) % side, (side - dz) % side
        for offset in ((dx, dz), (back_x, back_z), (dz, back_x), (back_z, dx)):
            if offset not in order and any(offset):
                order.append(offset)
    return order


def halves_of(x):
    high = x.astype(jnp.bfloat16)
    return high, (x - high.astype(jnp.float32)).astype(jnp.bfloat16)


def three_products(x, across):
    high, low = halves_of(x)
    return jnp.concatenate([high, low, high] if across else [high, high, low], axis=1)


def truncate(
    side,
    scale,
    slab_ref,
    start_ref,
    out_ref,
    basis_ref,
    slab,
    acc,
    part,
    pair,
    mine,
    arrived,
    line,
    whole,
    rows_ref,
    product_ref,
    m_ref,
    v_ref,
    spread_ref,
    moved,
    staged,
    load_sem,
    store_sem,
    own_sem,
    sum_send,
    sum_recv,
    row_send,
    row_recv,
):
    y, x, z, core = (lax.axis_index(name) for name in AXES)
    columns = acc.shape[0]
    tiles = columns // TILE
    blocks = [(i, j) for i in range(tiles) for j in range(i, tiles)]
    half = len(blocks) // 2
    count = slab_ref.shape[0]
    held = moved.shape[0]
    depth = count // CHUNKS

    loads = [
        pltpu.make_async_copy(slab_ref.at[pl.ds(n * depth, depth)], slab.at[n], load_sem.at[n]) for n in range(CHUNKS)
    ]
    for load in loads:
        load.start()

    def chip(offset):
        step_x, step_z = (step + core * ((side - step) % side - step) for step in offset)
        return lax.rem(x + step_x, side), lax.rem(z + step_z, side)

    plane = [chip(offset) for offset in far_first(side)]
    partner = (y, x, z, 1 - core)
    near = [(y, *to, core) for to in plane]
    peers = [(y, *to, c) for to in plane for c in (core, 1 - core)] + [partner]
    above = [(lax.rem(y + dy, side), x, z, core) for dy in range(1, side)]

    barrier = pltpu.get_barrier_semaphore()
    for to in peers + above:
        pl.semaphore_signal(barrier, inc=1, device_id=dict(zip(AXES, to)), device_id_type=MESH)

    def rows_of(index, size):
        return pl.ds(pl.multiple_of(index * size, size), size)

    def number(to):
        return (to[1] * side + to[2]) * 2 + to[3]

    me = number((y, x, z, core))
    place = x * side + z
    exchange = [
        [
            pltpu.make_async_remote_copy(
                src_ref=slab_ref.at[:, number(to) * held + i, :],
                dst_ref=moved.at[i, rows_of(me, count), :],
                send_sem=row_send.at[n, i],
                recv_sem=row_recv.at[n, i],
                device_id=dict(zip(AXES, to)),
                device_id_type=MESH,
            )
            for i in range(held)
        ]
        for n, to in enumerate(peers)
    ]
    kept = [
        pltpu.make_async_copy(slab_ref.at[:, me * held + i, :], moved.at[i, rows_of(me, count), :], own_sem.at[i])
        for i in range(held)
    ]

    def start(copies):
        for copy in copies:
            copy.start()

    for n in range(CHUNKS):
        if n == CHUNKS // 2:
            pl.semaphore_wait(barrier, len(peers + above))
            start(kept)
            for copies in exchange[len(peers) - EARLY :]:
                start(copies)
        loads[n].wait()
        high, low = halves_of(slab[n].reshape(-1, columns))
        left = jnp.concatenate([high, high, low], axis=0)
        right = jnp.concatenate([high, low, high], axis=0)
        for lo in range(0, columns, 256):
            new = lax.dot_general(
                left[:, : lo + 256], right[:, lo : lo + 256], (((0,), (0,)), ((), ())), preferred_element_type=jnp.float32
            )
            if n:
                new = acc[: lo + 256, lo : lo + 256] + new
            acc[: lo + 256, lo : lo + 256] = new
    for n, (i, j) in enumerate(blocks):
        part[n] = acc[i * TILE : (i + 1) * TILE, j * TILE : (j + 1) * TILE] * scale

    slots = iter(range(sum_send.shape[0]))

    def send(src, dst, to):
        slot = next(slots)
        copy = pltpu.make_async_remote_copy(
            src_ref=src,
            dst_ref=dst,
            send_sem=sum_send.at[slot],
            recv_sem=sum_recv.at[slot],
            device_id=dict(zip(AXES, to)),
            device_id_type=MESH,
        )
        copy.start()
        return copy

    send(part.at[pl.ds((1 - core) * half, half)], pair, partner).wait()
    own_half = pl.ds(core * half, half)
    mine[...] = part[own_half] + pair[...]

    copies = [
        send(mine.at[:, rows_of(to[1] * side + to[2], 8), :], arrived.at[n], to) for n, to in enumerate(near)
    ]
    total = mine[:, rows_of(place, 8), :]
    for n, copy in enumerate(copies):
        copy.wait_recv()
        total = total + arrived[n]
    line[y] = total
    for copy in copies:
        copy.wait_send()

    copies = [send(line.at[y], line.at[y], to) for to in above]
    for group in exchange[:MIDDLE]:
        start(group)
    for copy in copies:
        copy.wait()
    total = line[0]
    for k in range(1, side):
        total = total + line[k]
    own = whole.at[own_half, rows_of(place, 8), :]
    own[...] = total

    copies = [send(own, own, to) for to in near]
    passed = [send(own, own, partner)]
    for offset, copy in zip(far_first(side), copies):
        copy.wait_recv()
        back = chip(tuple((side - step) % side for step in offset))
        piece = whole.at[own_half, rows_of(back[0] * side + back[1], 8), :]
        passed.append(send(piece, piece, partner))
    for copy in copies:
        copy.wait_send()
    for copy in passed:
        copy.wait()
    for group in exchange[MIDDLE : len(peers) - EARLY]:
        start(group)

    for n, (i, j) in enumerate(blocks):
        block = whole[n]
        acc[i * TILE : (i + 1) * TILE, j * TILE : (j + 1) * TILE] = block
        if i != j:
            acc[j * TILE : (j + 1) * TILE, i * TILE : (i + 1) * TILE] = block.T
    rows_ref[...] = start_ref[...].T

    def step(_, carry):
        product_ref[...] = contract(rows_ref[...], acc[...], 1, 0)
        m_ref[...] = contract(product_ref[...], product_ref[...], 1, 1)
        inverse_cholesky(m_ref, v_ref, spread_ref)
        rows_ref[...] = contract(v_ref[...], product_ref[...], 1, 0)
        return carry

    lax.fori_loop(0, ITERS, step, 0)
    basis = three_products(rows_ref[...], True)
    basis_ref[...] = rows_ref[...].T

    for copies in exchange + [kept]:
        for copy in copies:
            copy.wait()
    stores = []
    for i in range(held):
        for lo in range(0, moved.shape[1], STRIPE):
            n = len(stores)
            staged[n] = lax.dot_general(
                three_products(moved[i, lo : lo + STRIPE, :], False),
                basis,
                (((1,), (1,)), ((), ())),
                preferred_element_type=jnp.float32,
            )
            stores.append(pltpu.make_async_copy(staged.at[n], out_ref.at[i, pl.ds(lo, STRIPE), :], store_sem.at[n]))
            stores[n].start()
    for store in stores:
        store.wait()


def on_device(slab, start):
    count, points, columns = slab.shape
    rank = start.shape[1]
    side = lax.axis_size("grp")
    peers = lax.axis_size(DEV)
    held = points // peers
    scale = 1.0 / (count * points * side * peers)
    tiles = columns // TILE
    half = tiles * (tiles + 1) // 4
    stripes = held * count * peers // STRIPE
    slots = 1 + 3 * (side * side - 1) + side
    vmem = pl.BlockSpec(memory_space=pltpu.VMEM)
    hbm = pl.BlockSpec(memory_space=pl.ANY)

    def scratch(*shape):
        return pltpu.VMEM(shape, jnp.float32)

    return pl.pallas_call(
        functools.partial(truncate, side, scale),
        out_shape=(
            jax.ShapeDtypeStruct((held, count * peers, rank), jnp.float32),
            jax.ShapeDtypeStruct((columns, rank), jnp.float32),
        ),
        in_specs=[hbm, vmem],
        out_specs=(hbm, vmem),
        scratch_shapes=[
            scratch(CHUNKS, count // CHUNKS, points, columns),
            scratch(columns, columns),
            scratch(2 * half, TILE, TILE),
            scratch(half, TILE, TILE),
            scratch(half, TILE, TILE),
            scratch(side * side - 1, half, 8, TILE),
            scratch(side, half, 8, TILE),
            scratch(2 * half, TILE, TILE),
            scratch(rank, columns),
            scratch(rank, columns),
            scratch(rank, rank),
            scratch(rank, rank),
            scratch(PANEL + PANEL // 4, 8, 2 * BLOCK),
            scratch(held, count * peers, columns),
            scratch(stripes, STRIPE, rank),
            pltpu.SemaphoreType.DMA((CHUNKS,)),
            pltpu.SemaphoreType.DMA((stripes,)),
            pltpu.SemaphoreType.DMA((held,)),
            pltpu.SemaphoreType.DMA((slots,)),
            pltpu.SemaphoreType.DMA((slots,)),
            pltpu.SemaphoreType.DMA((peers - 1, held)),
            pltpu.SemaphoreType.DMA((peers - 1, held)),
        ],
        compiler_params=pltpu.CompilerParams(
            collective_id=0, has_side_effects=True, vmem_limit_bytes=40 * 1024 * 1024
        ),
        name="truncate",
    )(slab, start)


def solution(mesh):
    torus = Mesh(mesh.devices.reshape(mesh.shape["grp"], 4, 4, 2), AXES)
    return jax.shard_map(
        on_device,
        mesh=torus,
        in_specs=(P(AXES, None, None), P()),
        out_specs=(P(DEV, "grp", None), P()),
        check_vma=False,
    )
```

```python
import functools

import jax
import jax.numpy as jnp
from jax import lax
from jax.experimental import pallas as pl
from jax.experimental.pallas import tpu as pltpu
from jax.sharding import Mesh
from jax.sharding import PartitionSpec as P

ITERS = 4
DEV = ("dev_0", "dev_1", "dev_2")
AXES = ("grp", *DEV)
MESH = pl.DeviceIdType.MESH
HIGHEST = lax.Precision.HIGHEST
BLOCK = 64
PANEL = 16
TILE = 128
CHUNKS = 4
STRIPE = 256
DURING = (4,)
RAW = (2, 1)
LATE = (3,)


def contract(a, b, dim_a, dim_b):
    return lax.dot_general(
        a, b, (((dim_a,), (dim_b,)), ((), ())), precision=HIGHEST, preferred_element_type=jnp.float32
    )


def inverse_factor(block, spread_ref):
    size = block.shape[0]
    diagonal = lax.broadcasted_iota(jnp.int32, (size, size), 0) == lax.broadcasted_iota(jnp.int32, (size, size), 1)
    both = jnp.concatenate([block, diagonal.astype(jnp.float32)], axis=1)
    wide = (8, 2 * size)
    count = size // 8
    tiles = [both[8 * t : 8 * t + 8, :] for t in range(count)]
    row_of = lax.broadcasted_iota(jnp.int32, wide, 0)

    def over_rows(row):
        return jnp.broadcast_to(row, wide)

    for first in range(0, count, PANEL // 8):
        after = first + PANEL // 8
        cols = [
            [jnp.broadcast_to(tiles[u][:, 8 * first + c : 8 * first + c + 1], wide) for u in range(first, count)]
            for c in range(PANEL)
        ]
        for t in range(first, after):
            spread_ref[PANEL + t - first] = tiles[t]
        spread_ref[0] = cols[0][0]
        for t in range(1, PANEL // 8):
            spread_ref[PANEL + PANEL // 8 + t - 1] = cols[0][t]
        rows = [over_rows(spread_ref[PANEL + i // 8, i % 8 : i % 8 + 1, :]) for i in range(PANEL)]
        pivots, scaled = [], []
        for c in range(PANEL):
            def at(i):
                if c == 0:
                    slot = 0 if i < 8 else PANEL + PANEL // 8 + i // 8 - 1
                    return over_rows(spread_ref[slot, i % 8 : i % 8 + 1, :])
                return over_rows(cols[c][i // 8][i % 8 : i % 8 + 1, :])

            pivots.append(at(c))
            inverse = 1.0 / pivots[c]
            for k in range(c + 1, PANEL):
                factor = at(k) * inverse
                for u in range(k // 8, count - first):
                    cols[k][u] = cols[k][u] - factor * cols[c][u]
                rows[k] = rows[k] - factor * rows[c]
            scaled.append(rows[c] * inverse)
        for u in range(after, count):
            change = cols[0][u - first] * scaled[0]
            for c in range(1, PANEL):
                change = change + cols[c][u - first] * scaled[c]
            tiles[u] = tiles[u] - change
        for c in range(PANEL):
            t = first + c // 8
            tiles[t] = jnp.where(row_of == c % 8, rows[c] * lax.rsqrt(pivots[c]), tiles[t])
    return jnp.concatenate(tiles, axis=0)[:, size:]


def inverse_cholesky(m_ref, v_ref, spread_ref):
    size = m_ref.shape[0]
    v_ref[...] = jnp.zeros_like(v_ref)
    corner = m_ref[:BLOCK, :BLOCK]
    for lo in range(0, size, BLOCK):
        hi = lo + BLOCK
        end = min(hi + BLOCK, size)
        inner = inverse_factor(corner, spread_ref)
        if hi < size:
            across = contract(inner, m_ref[lo:hi, hi:end], 1, 0)
            down = contract(m_ref[hi:end, lo:hi], inner, 1, 1)
            corner = m_ref[hi:end, hi:end] - contract(down, across, 1, 0)
        if lo:
            v_ref[lo:hi, :lo] = contract(inner, v_ref[lo:hi, :lo], 1, 0)
        v_ref[lo:hi, lo:hi] = inner
        if end < size:
            far_across = contract(inner, m_ref[lo:hi, end:], 1, 0)
            far_down = contract(m_ref[end:, lo:hi], inner, 1, 1)
            m_ref[hi:end, end:] -= contract(down, far_across, 1, 0)
            m_ref[end:, hi:end] -= contract(far_down, across, 1, 0)
            m_ref[end:, end:] -= contract(far_down, far_across, 1, 0)
            v_ref[end:, :hi] -= contract(far_down, v_ref[lo:hi, :hi], 1, 0)
        if hi < size:
            v_ref[hi:end, :hi] -= contract(down, v_ref[lo:hi, :hi], 1, 0)


def offsets_at(side, distances):
    def hops(offset):
        return sum(min(step, side - step) for step in offset)

    order = []
    for distance in distances:
        for dx in range(side):
            for dz in range(side):
                if hops((dx, dz)) != distance:
                    continue
                back_x, back_z = (side - dx) % side, (side - dz) % side
                for offset in ((dx, dz), (back_x, back_z), (dz, back_x), (back_z, dx)):
                    if offset not in order:
                        order.append(offset)
    return order


def halves_of(x):
    high = x.astype(jnp.bfloat16)
    return high, (x - high.astype(jnp.float32)).astype(jnp.bfloat16)


def three_products(x, across):
    high, low = halves_of(x)
    return jnp.concatenate([high, low, high] if across else [high, high, low], axis=1)


def truncate(
    side,
    scale,
    slab_ref,
    start_ref,
    moved,
    rows_ref,
    v_ref,
    slab,
    acc,
    part,
    pair,
    mine,
    first_in,
    partial,
    second_in,
    line,
    whole,
    start_held,
    product_ref,
    m_ref,
    spread_ref,
    late_rows,
    late_out,
    load_sem,
    own_sem,
    late_sem,
    sum_send,
    sum_recv,
    row_send,
    row_recv,
):
    y, x, z, core = (lax.axis_index(name) for name in AXES)
    rank, columns = rows_ref.shape
    tiles = columns // TILE
    blocks = [(i, j) for i in range(tiles) for j in range(i, tiles)]
    half = len(blocks) // 2
    count = slab_ref.shape[0]
    held = moved.shape[0]
    depth = count // CHUNKS
    wide = TILE // side
    thin = wide // side

    loads = [
        pltpu.make_async_copy(slab_ref.at[pl.ds(n * depth, depth)], slab.at[n], load_sem.at[n]) for n in range(CHUNKS)
    ]
    loads.append(pltpu.make_async_copy(start_ref, start_held, load_sem.at[CHUNKS]))
    for load in loads:
        load.start()

    first, second = x + core * (z - x), z + core * (x - z)

    def in_plane(f, s):
        return f + core * (s - f), s + core * (f - s)

    steps = range(1, side)
    along_first = [(y, *in_plane(lax.rem(first + k, side), second), core) for k in steps]
    along_second = [(y, *in_plane(first, lax.rem(second + k, side)), core) for k in steps]
    along_y = [(lax.rem(y + k, side), x, z, core) for k in steps]
    partner = (y, x, z, 1 - core)

    barrier = pltpu.get_barrier_semaphore()
    greeted = [*along_first, *along_second, *along_y, partner]
    for to in greeted:
        pl.semaphore_signal(barrier, inc=1, device_id=dict(zip(AXES, to)), device_id_type=MESH)

    def rows_of(index, size):
        return pl.ds(pl.multiple_of(index * size, size), size)

    def number(to):
        return (to[1] * side + to[2]) * 2 + to[3]

    me = number((y, x, z, core))

    def chip(offset):
        step_x, step_z = (step + core * ((side - step) % side - step) for step in offset)
        return lax.rem(x + step_x, side), lax.rem(z + step_z, side)

    def both_cores(distances):
        return [(y, *chip(offset), c) for offset in offsets_at(side, distances) for c in (core, 1 - core)]

    groups = {name: both_cores(name) for name in (DURING, RAW, LATE)}
    groups[()] = [partner]
    exchange, kept, late = {}, [], []
    slot = 0
    for name, peers in groups.items():
        exchange[name] = []
        for n, to in enumerate(peers):
            for i in range(held):
                point = number(to) * held + i
                src, dst = slab_ref.at[:, point, :], moved.at[i, rows_of(me, count), :]
                if name == LATE:
                    place = pl.ds((n * held + i) * count, count)
                    late.append(pltpu.make_async_copy(src, late_rows.at[place], late_sem.at[n, i]))
                    src, dst = late_out.at[place], moved.at[i, rows_of(me, count), pl.ds(0, rank)]
                exchange[name].append(
                    pltpu.make_async_remote_copy(
                        src_ref=src,
                        dst_ref=dst,
                        send_sem=row_send.at[slot, i],
                        recv_sem=row_recv.at[slot, i],
                        device_id=dict(zip(AXES, to)),
                        device_id_type=MESH,
                    )
                )
            slot += 1
    for i in range(held):
        kept.append(
            pltpu.make_async_copy(slab_ref.at[:, me * held + i, :], moved.at[i, rows_of(me, count), :], own_sem.at[i])
        )

    def start(copies):
        for copy in copies:
            copy.start()

    for n in range(CHUNKS):
        loads[n].wait()
        high, low = halves_of(slab[n].reshape(-1, columns))
        for left, right, rows, lo in (
            (high[:, :256], high[:, :256], 256, 0),
            (high, high[:, 256:], columns, 256),
            (high, low, columns, columns),
        ):
            new = lax.dot_general(left, right, (((0,), (0,)), ((), ())), preferred_element_type=jnp.float32)
            place = (slice(0, rows), slice(lo, lo + new.shape[1]))
            acc[place] = acc[place] + new if n else new
    for n, (i, j) in enumerate(blocks):
        across = acc[i * TILE : (i + 1) * TILE, columns + j * TILE : columns + (j + 1) * TILE]
        down = acc[j * TILE : (j + 1) * TILE, columns + i * TILE : columns + (i + 1) * TILE]
        part[n] = (acc[i * TILE : (i + 1) * TILE, j * TILE : (j + 1) * TILE] + (across + down.T)) * scale
    pl.semaphore_wait(barrier, len(greeted))

    slots = iter(range(sum_send.shape[0]))

    def send(src, dst, to):
        slot = next(slots)
        copy = pltpu.make_async_remote_copy(
            src_ref=src,
            dst_ref=dst,
            send_sem=sum_send.at[slot],
            recv_sem=sum_recv.at[slot],
            device_id=dict(zip(AXES, to)),
            device_id_type=MESH,
        )
        copy.start()
        return copy

    def wait(copies):
        for copy in copies:
            copy.wait()

    send(part.at[pl.ds((1 - core) * half, half)], pair, partner).wait()
    own_half = pl.ds(core * half, half)
    mine[...] = part[own_half] + pair[...]

    copies = [
        send(mine.at[:, rows_of(lax.rem(first + k, side), wide), :], first_in.at[k - 1], to)
        for k, to in zip(steps, along_first)
    ]
    start(kept + exchange[()] + late)
    wait(copies)
    partial[...] = mine[:, rows_of(first, wide), :] + (first_in[0] + sum(first_in[k] for k in range(1, side - 1)))
    copies = [
        send(partial.at[:, rows_of(lax.rem(second + k, side), thin), :], second_in.at[k - 1], to)
        for k, to in zip(steps, along_second)
    ]
    wait(copies)
    line[y] = partial[:, rows_of(second, thin), :] + (
        second_in[0] + sum(second_in[k] for k in range(1, side - 1))
    )

    copies = [send(line.at[y], line.at[y], to) for to in along_y]
    start(exchange[DURING])
    wait(copies)
    total = line[0]
    for k in steps:
        total = total + line[k]
    own = whole.at[own_half, rows_of(first * side + second, thin), :]
    own[...] = total

    wait([send(own, own, to) for to in along_second])

    def strip(f):
        return whole.at[own_half, rows_of(f, wide), :]

    copies = [send(strip(first), strip(first), to) for to in along_first]
    passed = [send(strip(first), strip(first), partner)]
    for k, copy in zip(steps, copies):
        copy.wait_recv()
        piece = strip(lax.rem(first + side - k, side))
        passed.append(send(piece, piece, partner))
    for copy in copies:
        copy.wait_send()
    start(exchange[RAW])
    wait(passed)

    for n, (i, j) in enumerate(blocks):
        block = whole[n]
        acc[i * TILE : (i + 1) * TILE, j * TILE : (j + 1) * TILE] = block
        if i != j:
            acc[j * TILE : (j + 1) * TILE, i * TILE : (i + 1) * TILE] = block.T
    loads[CHUNKS].wait()
    rows_ref[...] = start_held[...].T

    def step(k, carry):
        product_ref[...] = contract(rows_ref[...], acc[:, :columns], 1, 0)

        @pl.when(k == ITERS - 1)
        def _():
            wait(late)
            late_out[...] = contract(late_rows[...], product_ref[...], 1, 1)
            start(exchange[LATE])

        m_ref[...] = contract(product_ref[...], product_ref[...], 1, 1)
        inverse_cholesky(m_ref, v_ref, spread_ref)
        rows_ref[...] = contract(v_ref[...], product_ref[...], 1, 0)
        return carry

    lax.fori_loop(0, ITERS, step, 0)
    for copies in exchange.values():
        wait(copies)
    wait(kept)


def project(side, moved_ref, rows_ref, v_ref, out_ref, basis_ref, staged, turned, store_sem):
    x, z = (lax.axis_index(name) for name in DEV[:2])
    held, count, rank = staged.shape
    turned[...] = rows_ref[...].T
    stores = [pltpu.make_async_copy(turned, basis_ref, store_sem.at[0])]
    stores[0].start()
    basis = three_products(rows_ref[...], True)
    stripes = [(i, pl.ds(lo, STRIPE)) for i in range(held) for lo in range(0, count, STRIPE)]
    for i, rows in stripes:
        staged[i, rows, :] = lax.dot_general(
            three_products(moved_ref[i, rows, :], False),
            basis,
            (((1,), (1,)), ((), ())),
            preferred_element_type=jnp.float32,
        )
    size = count // (side * side)
    places = []
    for dx, dz in offsets_at(side, LATE):
        chip = lax.rem(x + dx, side) * side + lax.rem(z + dz, side)
        places += [(i, pl.ds(pl.multiple_of(chip * size, size), size)) for i in range(held)]
    late = jnp.concatenate([moved_ref[i, rows, :rank] for i, rows in places], axis=0)
    late = contract(late, v_ref[...], 1, 1)
    for n, (i, rows) in enumerate(places):
        staged[i, rows, :] = late[n * size : (n + 1) * size]
    for n, (i, rows) in enumerate(stripes):
        stores.append(pltpu.make_async_copy(staged.at[i, rows, :], out_ref.at[i, rows, :], store_sem.at[n + 1]))
        stores[-1].start()
    for store in stores:
        store.wait()


def on_device(slab, start):
    count, points, columns = slab.shape
    rank = start.shape[1]
    side = lax.axis_size("grp")
    peers = lax.axis_size(DEV)
    held = points // peers
    scale = 1.0 / (count * points * side * peers)
    tiles = columns // TILE
    half = tiles * (tiles + 1) // 4
    late = 2 * len(offsets_at(side, LATE))
    slots = 1 + 5 * (side - 1) + side
    vmem = pl.BlockSpec(memory_space=pltpu.VMEM)
    hbm = pl.BlockSpec(memory_space=pltpu.HBM)

    def scratch(*shape):
        return pltpu.VMEM(shape, jnp.float32)

    moved, rows, factor = pl.pallas_call(
        functools.partial(truncate, side, scale),
        out_shape=(
            jax.ShapeDtypeStruct((held, count * peers, columns), jnp.float32),
            jax.ShapeDtypeStruct((rank, columns), jnp.float32),
            jax.ShapeDtypeStruct((rank, rank), jnp.float32),
        ),
        in_specs=[hbm, hbm],
        out_specs=(vmem, vmem, vmem),
        scratch_shapes=[
            scratch(CHUNKS, count // CHUNKS, points, columns),
            scratch(columns, 2 * columns),
            scratch(2 * half, TILE, TILE),
            scratch(half, TILE, TILE),
            scratch(half, TILE, TILE),
            scratch(side - 1, half, TILE // side, TILE),
            scratch(half, TILE // side, TILE),
            scratch(side - 1, half, TILE // side**2, TILE),
            scratch(side, half, TILE // side**2, TILE),
            scratch(2 * half, TILE, TILE),
            scratch(columns, rank),
            scratch(rank, columns),
            scratch(rank, rank),
            scratch(PANEL + PANEL // 4, 8, 2 * BLOCK),
            scratch(late * held * count, columns),
            scratch(late * held * count, rank),
            pltpu.SemaphoreType.DMA((CHUNKS + 1,)),
            pltpu.SemaphoreType.DMA((held,)),
            pltpu.SemaphoreType.DMA((late, held)),
            pltpu.SemaphoreType.DMA((slots,)),
            pltpu.SemaphoreType.DMA((slots,)),
            pltpu.SemaphoreType.DMA((peers - 1, held)),
            pltpu.SemaphoreType.DMA((peers - 1, held)),
        ],
        compiler_params=pltpu.CompilerParams(
            collective_id=0, has_side_effects=True, vmem_limit_bytes=47 * 1024 * 1024
        ),
        name="truncate",
    )(slab, start)
    return pl.pallas_call(
        functools.partial(project, side),
        out_shape=(
            jax.ShapeDtypeStruct((held, count * peers, rank), jnp.float32),
            jax.ShapeDtypeStruct((columns, rank), jnp.float32),
        ),
        in_specs=[vmem, vmem, vmem],
        out_specs=(hbm, hbm),
        scratch_shapes=[
            scratch(held, count * peers, rank),
            scratch(columns, rank),
            pltpu.SemaphoreType.DMA((1 + held * count * peers // STRIPE,)),
        ],
        compiler_params=pltpu.CompilerParams(vmem_limit_bytes=24 * 1024 * 1024),
        name="project",
    )(moved, rows, factor)


def solution(mesh):
    torus = Mesh(mesh.devices.reshape(mesh.shape["grp"], 4, 4, 2), AXES)
    return jax.shard_map(
        on_device,
        mesh=torus,
        in_specs=(P(AXES, None, None), P()),
        out_specs=(P(DEV, "grp", None), P()),
        check_vma=False,
    )
```

```python
import functools

import jax
import jax.numpy as jnp
from jax import lax
from jax.experimental import pallas as pl
from jax.experimental.pallas import tpu as pltpu
from jax.sharding import Mesh
from jax.sharding import PartitionSpec as P

ITERS = 4
DEV = ("dev_0", "dev_1", "dev_2")
AXES = ("grp", *DEV)
MESH = pl.DeviceIdType.MESH
HIGHEST = lax.Precision.HIGHEST
BLOCK = 64
PANEL = 16
TILE = 128
CHUNKS = 4
STRIPE = 256


def short_contract(a, b, dim_a, dim_b):
    (a, a_low), (b, b_low) = halves_of(a), halves_of(b)
    dims = (((dim_a,), (dim_b,)), ((), ()))
    products = [lax.dot_general(p, q, dims, preferred_element_type=jnp.float32) for p, q in ((a, b), (a, b_low), (a_low, b))]
    return products[0] + (products[1] + products[2])


def contract(a, b, dim_a, dim_b):
    return lax.dot_general(
        a, b, (((dim_a,), (dim_b,)), ((), ())), precision=HIGHEST, preferred_element_type=jnp.float32
    )


def inverse_factor(block, spread_ref):
    size = block.shape[0]
    diagonal = lax.broadcasted_iota(jnp.int32, (size, size), 0) == lax.broadcasted_iota(jnp.int32, (size, size), 1)
    both = jnp.concatenate([block, diagonal.astype(jnp.float32)], axis=1)
    wide = (8, 2 * size)
    count = size // 8
    tiles = [both[8 * t : 8 * t + 8, :] for t in range(count)]
    row_of = lax.broadcasted_iota(jnp.int32, wide, 0)

    def over_rows(row):
        return jnp.broadcast_to(row, wide)

    for first in range(0, count, PANEL // 8):
        after = first + PANEL // 8
        cols = [
            [jnp.broadcast_to(tiles[u][:, 8 * first + c : 8 * first + c + 1], wide) for u in range(first, count)]
            for c in range(PANEL)
        ]
        for t in range(first, after):
            spread_ref[PANEL + t - first] = tiles[t]
        spread_ref[0] = cols[0][0]
        for t in range(1, PANEL // 8):
            spread_ref[PANEL + PANEL // 8 + t - 1] = cols[0][t]
        rows = [over_rows(spread_ref[PANEL + i // 8, i % 8 : i % 8 + 1, :]) for i in range(PANEL)]
        pivots, scaled = [], []
        for c in range(PANEL):
            def at(i):
                if c == 0:
                    slot = 0 if i < 8 else PANEL + PANEL // 8 + i // 8 - 1
                    return over_rows(spread_ref[slot, i % 8 : i % 8 + 1, :])
                return over_rows(cols[c][i // 8][i % 8 : i % 8 + 1, :])

            pivots.append(at(c))
            inverse = 1.0 / pivots[c]
            for k in range(c + 1, PANEL):
                factor = at(k) * inverse
                for u in range(k // 8, count - first):
                    cols[k][u] = cols[k][u] - factor * cols[c][u]
                rows[k] = rows[k] - factor * rows[c]
            scaled.append(rows[c] * inverse)
        for u in range(after, count):
            change = cols[0][u - first] * scaled[0]
            for c in range(1, PANEL):
                change = change + cols[c][u - first] * scaled[c]
            tiles[u] = tiles[u] - change
        for c in range(PANEL):
            t = first + c // 8
            tiles[t] = jnp.where(row_of == c % 8, rows[c] * lax.rsqrt(pivots[c]), tiles[t])
    return jnp.concatenate(tiles, axis=0)[:, size:]


def inverse_cholesky(m_ref, v_ref, spread_ref):
    size = m_ref.shape[0]
    v_ref[...] = jnp.zeros_like(v_ref)
    corner = m_ref[:BLOCK, :BLOCK]
    for lo in range(0, size, BLOCK):
        hi = lo + BLOCK
        end = min(hi + BLOCK, size)
        inner = inverse_factor(corner, spread_ref)
        if hi < size:
            across = contract(inner, m_ref[lo:hi, hi:end], 1, 0)
            down = contract(m_ref[hi:end, lo:hi], inner, 1, 1)
            corner = m_ref[hi:end, hi:end] - contract(down, across, 1, 0)
        if lo:
            v_ref[lo:hi, :lo] = contract(inner, v_ref[lo:hi, :lo], 1, 0)
        v_ref[lo:hi, lo:hi] = inner
        if end < size:
            far_across = contract(inner, m_ref[lo:hi, end:], 1, 0)
            far_down = contract(m_ref[end:, lo:hi], inner, 1, 1)
            m_ref[hi:end, end:] -= contract(down, far_across, 1, 0)
            m_ref[end:, hi:end] -= contract(far_down, across, 1, 0)
            m_ref[end:, end:] -= contract(far_down, far_across, 1, 0)
            v_ref[end:, :hi] -= contract(far_down, v_ref[lo:hi, :hi], 1, 0)
        if hi < size:
            v_ref[hi:end, :hi] -= contract(down, v_ref[lo:hi, :hi], 1, 0)


def offsets_at(side, distance):
    order = []
    for dx in range(side):
        for dz in range(side):
            if min(dx, side - dx) + min(dz, side - dz) != distance:
                continue
            back_x, back_z = (side - dx) % side, (side - dz) % side
            for offset in ((dx, dz), (back_x, back_z), (dz, back_x), (back_z, dx)):
                if offset not in order:
                    order.append(offset)
    return order


def late_offsets(side):
    return [(offset, 0) for offset in offsets_at(side, 3)] + [(offset, 1) for offset in offsets_at(side, 4)]


def raw_offsets(side):
    every = [(offset, flip) for d in (4, 3, 2, 1) for offset in offsets_at(side, d) for flip in range(2)]
    return [(offset, flip) for offset, flip in every if (offset, flip) not in late_offsets(side)]


def halves_of(x):
    high = x.astype(jnp.bfloat16)
    return high, (x - high.astype(jnp.float32)).astype(jnp.bfloat16)


def three_products(x, across):
    high, low = halves_of(x)
    return jnp.concatenate([high, low, high] if across else [high, high, low], axis=1)


def truncate(
    side,
    scale,
    slab_ref,
    start_ref,
    moved,
    rows_ref,
    v_ref,
    slab,
    acc,
    part,
    pair,
    mine,
    first_in,
    partial,
    slices,
    whole,
    start_held,
    product_ref,
    m_ref,
    spread_ref,
    late_rows,
    late_out,
    load_sem,
    own_sem,
    late_sem,
    sum_send,
    sum_recv,
    row_send,
    row_recv,
):
    y, x, z, core = (lax.axis_index(name) for name in AXES)
    rank, columns = rows_ref.shape
    tiles = columns // TILE
    blocks = [(i, j) for i in range(tiles) for j in range(i, tiles)]
    half = len(blocks) // 2
    count = slab_ref.shape[0]
    held = moved.shape[0]
    depth = count // CHUNKS
    wide = TILE // side
    thin = wide // side

    loads = [
        pltpu.make_async_copy(slab_ref.at[pl.ds(n * depth, depth)], slab.at[n], load_sem.at[n]) for n in range(CHUNKS)
    ]
    loads.append(pltpu.make_async_copy(start_ref, start_held, load_sem.at[CHUNKS]))
    for load in loads:
        load.start()

    first, second = x + core * (z - x), z + core * (x - z)

    def in_plane(f, s):
        return f + core * (s - f), s + core * (f - s)

    steps = range(1, side)
    along_first = [(y, *in_plane(lax.rem(first + k, side), second), core) for k in steps]
    along_second = [(y, *in_plane(first, lax.rem(second + k, side)), core) for k in steps]
    around = [(ky, ks) for ky in range(side) for ks in range(side) if ky or ks]
    crossing = [(lax.rem(y + ky, side), *in_plane(first, lax.rem(second + ks, side)), core) for ky, ks in around]
    partner = (y, x, z, 1 - core)

    barrier = pltpu.get_barrier_semaphore()
    greeted = [*along_first, *crossing, partner]
    for to in greeted:
        pl.semaphore_signal(barrier, inc=1, device_id=dict(zip(AXES, to)), device_id_type=MESH)

    def rows_of(index, size):
        return pl.ds(pl.multiple_of(index * size, size), size)

    def number(to):
        return (to[1] * side + to[2]) * 2 + to[3]

    me = number((y, x, z, core))

    def chip(offset):
        step_x, step_z = (step + core * ((side - step) % side - step) for step in offset)
        return lax.rem(x + step_x, side), lax.rem(z + step_z, side)

    def devices(offsets):
        return [(y, *chip(offset), core + flip * (1 - 2 * core)) for offset, flip in offsets]

    groups = {"near": [partner], "raw": devices(raw_offsets(side)), "late": devices(late_offsets(side))}
    exchange, kept, late = {}, [], []
    slot = 0
    for name, peers in groups.items():
        exchange[name] = []
        for n, to in enumerate(peers):
            for i in range(held):
                point = number(to) * held + i
                src, dst = slab_ref.at[:, point, :], moved.at[i, rows_of(me, count), :]
                if name == "late":
                    place = pl.ds((n * held + i) * count, count)
                    late.append(pltpu.make_async_copy(src, late_rows.at[place], late_sem.at[n, i]))
                    src, dst = late_out.at[place], moved.at[i, rows_of(me, count), pl.ds(0, rank)]
                exchange[name].append(
                    pltpu.make_async_remote_copy(
                        src_ref=src,
                        dst_ref=dst,
                        send_sem=row_send.at[slot, i],
                        recv_sem=row_recv.at[slot, i],
                        device_id=dict(zip(AXES, to)),
                        device_id_type=MESH,
                    )
                )
            slot += 1
    for i in range(held):
        kept.append(
            pltpu.make_async_copy(slab_ref.at[:, me * held + i, :], moved.at[i, rows_of(me, count), :], own_sem.at[i])
        )

    def start(copies):
        for copy in copies:
            copy.start()

    for n in range(CHUNKS):
        loads[n].wait()
        high, low = halves_of(slab[n].reshape(-1, columns))
        for left, right, rows, lo in (
            (high[:, :256], high[:, :256], 256, 0),
            (high, high[:, 256:], columns, 256),
            (high, low, columns, columns),
        ):
            new = lax.dot_general(left, right, (((0,), (0,)), ((), ())), preferred_element_type=jnp.float32)
            place = (slice(0, rows), slice(lo, lo + new.shape[1]))
            acc[place] = acc[place] + new if n else new
    for n, (i, j) in enumerate(blocks):
        across = acc[i * TILE : (i + 1) * TILE, columns + j * TILE : columns + (j + 1) * TILE]
        down = acc[j * TILE : (j + 1) * TILE, columns + i * TILE : columns + (i + 1) * TILE]
        part[n] = (acc[i * TILE : (i + 1) * TILE, j * TILE : (j + 1) * TILE] + (across + down.T)) * scale
    pl.semaphore_wait(barrier, len(greeted))

    sent = []

    def send(src, dst, to):
        slot = len(sent)
        sent.append(
            pltpu.make_async_remote_copy(
                src_ref=src,
                dst_ref=dst,
                send_sem=sum_send.at[slot],
                recv_sem=sum_recv.at[slot],
                device_id=dict(zip(AXES, to)),
                device_id_type=MESH,
            )
        )
        sent[slot].start()
        return sent[slot]

    def arrive(copies):
        for copy in copies:
            copy.wait_recv()

    def wait(copies):
        for copy in copies:
            copy.wait()

    arrive([send(part.at[pl.ds((1 - core) * half, half)], pair, partner)])
    own_half = pl.ds(core * half, half)
    mine[...] = part[own_half] + pair[...]

    copies = [
        send(mine.at[:, rows_of(lax.rem(first + k, side), wide), :], first_in.at[k - 1], to)
        for k, to in zip(steps, along_first)
    ]
    start(kept + exchange["near"] + late)
    arrive(copies)
    partial[...] = mine[:, rows_of(first, wide), :] + (first_in[0] + sum(first_in[k] for k in range(1, side - 1)))
    source = y * side + second
    copies = [
        send(partial.at[:, rows_of(lax.rem(second + ks, side), thin), :], slices.at[source], to)
        for (_, ks), to in zip(around, crossing)
    ]
    slices[source] = partial[:, rows_of(second, thin), :]
    arrive(copies)
    total = slices[0]
    for k in range(1, side * side):
        total = total + slices[k]
    own = whole.at[own_half, rows_of(first * side + second, thin), :]
    own[...] = total

    arrive([send(own, own, to) for to in along_second])

    def strip(f):
        return whole.at[own_half, rows_of(f, wide), :]

    copies = [send(strip(first), strip(first), to) for to in along_first]
    passed = [send(strip(first), strip(first), partner)]
    for k, copy in zip(steps, copies):
        copy.wait_recv()
        piece = strip(lax.rem(first + side - k, side))
        passed.append(send(piece, piece, partner))
    start(exchange["raw"])
    arrive(passed)

    for n, (i, j) in enumerate(blocks):
        block = whole[n]
        acc[i * TILE : (i + 1) * TILE, j * TILE : (j + 1) * TILE] = block
        if i != j:
            acc[j * TILE : (j + 1) * TILE, i * TILE : (i + 1) * TILE] = block.T
    loads[CHUNKS].wait()
    rows_ref[...] = start_held[...].T

    def step(k, carry):
        product_ref[...] = contract(rows_ref[...], acc[:, :columns], 1, 0)

        @pl.when(k == ITERS - 1)
        def _():
            wait(late)
            late_out[...] = short_contract(late_rows[...], product_ref[...], 1, 1)
            start(exchange["late"])

        m_ref[...] = short_contract(product_ref[...], product_ref[...], 1, 1)
        inverse_cholesky(m_ref, v_ref, spread_ref)
        rows_ref[...] = short_contract(v_ref[...], product_ref[...], 1, 0)
        return carry

    lax.fori_loop(0, ITERS, step, 0)
    for copies in exchange.values():
        wait(copies)
    wait(kept)
    for copy in sent:
        copy.wait_send()


def project(side, moved_ref, rows_ref, v_ref, out_ref, basis_ref, staged, turned, store_sem):
    x, z, core = (lax.axis_index(name) for name in DEV)
    held, count, rank = staged.shape
    turned[...] = rows_ref[...].T
    stores = [pltpu.make_async_copy(turned, basis_ref, store_sem.at[0])]
    stores[0].start()
    basis = three_products(rows_ref[...], True)
    stripes = [(i, pl.ds(lo, STRIPE)) for i in range(held) for lo in range(0, count, STRIPE)]
    for i, rows in stripes:
        staged[i, rows, :] = lax.dot_general(
            three_products(moved_ref[i, rows, :], False),
            basis,
            (((1,), (1,)), ((), ())),
            preferred_element_type=jnp.float32,
        )
    size = count // (2 * side * side)
    places = []
    for (dx, dz), flip in late_offsets(side):
        chip = lax.rem(x + dx, side) * side + lax.rem(z + dz, side)
        device = 2 * chip + core + flip * (1 - 2 * core)
        places += [(i, pl.ds(pl.multiple_of(device * size, size), size)) for i in range(held)]
    late = jnp.concatenate([moved_ref[i, rows, :rank] for i, rows in places], axis=0)
    late = short_contract(late, v_ref[...], 1, 1)
    for n, (i, rows) in enumerate(places):
        staged[i, rows, :] = late[n * size : (n + 1) * size]
    for n, (i, rows) in enumerate(stripes):
        stores.append(pltpu.make_async_copy(staged.at[i, rows, :], out_ref.at[i, rows, :], store_sem.at[n + 1]))
        stores[-1].start()
    for store in stores:
        store.wait()


def on_device(slab, start):
    count, points, columns = slab.shape
    rank = start.shape[1]
    side = lax.axis_size("grp")
    peers = lax.axis_size(DEV)
    held = points // peers
    scale = 1.0 / (count * points * side * peers)
    tiles = columns // TILE
    half = tiles * (tiles + 1) // 4
    late = len(late_offsets(side))
    slots = side * side + 3 * (side - 1) + side
    vmem = pl.BlockSpec(memory_space=pltpu.VMEM)
    hbm = pl.BlockSpec(memory_space=pltpu.HBM)

    def scratch(*shape):
        return pltpu.VMEM(shape, jnp.float32)

    moved, rows, factor = pl.pallas_call(
        functools.partial(truncate, side, scale),
        out_shape=(
            jax.ShapeDtypeStruct((held, count * peers, columns), jnp.float32),
            jax.ShapeDtypeStruct((rank, columns), jnp.float32),
            jax.ShapeDtypeStruct((rank, rank), jnp.float32),
        ),
        in_specs=[hbm, hbm],
        out_specs=(vmem, vmem, vmem),
        scratch_shapes=[
            scratch(CHUNKS, count // CHUNKS, points, columns),
            scratch(columns, 2 * columns),
            scratch(2 * half, TILE, TILE),
            scratch(half, TILE, TILE),
            scratch(half, TILE, TILE),
            scratch(side - 1, half, TILE // side, TILE),
            scratch(half, TILE // side, TILE),
            scratch(side * side, half, TILE // side**2, TILE),
            scratch(2 * half, TILE, TILE),
            scratch(columns, rank),
            scratch(rank, columns),
            scratch(rank, rank),
            scratch(PANEL + PANEL // 4, 8, 2 * BLOCK),
            scratch(late * held * count, columns),
            scratch(late * held * count, rank),
            pltpu.SemaphoreType.DMA((CHUNKS + 1,)),
            pltpu.SemaphoreType.DMA((held,)),
            pltpu.SemaphoreType.DMA((late, held)),
            pltpu.SemaphoreType.DMA((slots,)),
            pltpu.SemaphoreType.DMA((slots,)),
            pltpu.SemaphoreType.DMA((peers - 1, held)),
            pltpu.SemaphoreType.DMA((peers - 1, held)),
        ],
        compiler_params=pltpu.CompilerParams(
            collective_id=0, has_side_effects=True, vmem_limit_bytes=47 * 1024 * 1024
        ),
        name="truncate",
    )(slab, start)
    return pl.pallas_call(
        functools.partial(project, side),
        out_shape=(
            jax.ShapeDtypeStruct((held, count * peers, rank), jnp.float32),
            jax.ShapeDtypeStruct((columns, rank), jnp.float32),
        ),
        in_specs=[vmem, vmem, vmem],
        out_specs=(hbm, hbm),
        scratch_shapes=[
            scratch(held, count * peers, rank),
            scratch(columns, rank),
            pltpu.SemaphoreType.DMA((1 + held * count * peers // STRIPE,)),
        ],
        compiler_params=pltpu.CompilerParams(vmem_limit_bytes=24 * 1024 * 1024),
        name="project",
    )(moved, rows, factor)


def solution(mesh):
    torus = Mesh(mesh.devices.reshape(mesh.shape["grp"], 4, 4, 2), AXES)
    return jax.shard_map(
        on_device,
        mesh=torus,
        in_specs=(P(AXES, None, None), P()),
        out_specs=(P(DEV, "grp", None), P()),
        check_vma=False,
    )
```

```python
import functools

import jax
import jax.numpy as jnp
from jax import lax
from jax.experimental import pallas as pl
from jax.experimental.pallas import tpu as pltpu
from jax.sharding import Mesh
from jax.sharding import PartitionSpec as P

ITERS = 4
DEV = ("dev_0", "dev_1", "dev_2")
AXES = ("grp", *DEV)
MESH = pl.DeviceIdType.MESH
HIGHEST = lax.Precision.HIGHEST
BLOCK = 64
PANEL = 16
TILE = 128
CHUNKS = 4
STRIPE = 256


def short_contract(a, b, dim_a, dim_b):
    (a, a_low), (b, b_low) = halves_of(a), halves_of(b)
    dims = (((dim_a,), (dim_b,)), ((), ()))
    products = [lax.dot_general(p, q, dims, preferred_element_type=jnp.float32) for p, q in ((a, b), (a, b_low), (a_low, b))]
    return products[0] + (products[1] + products[2])


def contract(a, b, dim_a, dim_b):
    return lax.dot_general(
        a, b, (((dim_a,), (dim_b,)), ((), ())), precision=HIGHEST, preferred_element_type=jnp.float32
    )


def inverse_factor(block, spread_ref):
    size = block.shape[0]
    diagonal = lax.broadcasted_iota(jnp.int32, (size, size), 0) == lax.broadcasted_iota(jnp.int32, (size, size), 1)
    both = jnp.concatenate([block, diagonal.astype(jnp.float32)], axis=1)
    wide = (8, 2 * size)
    count = size // 8
    tiles = [both[8 * t : 8 * t + 8, :] for t in range(count)]
    row_of = lax.broadcasted_iota(jnp.int32, wide, 0)

    def over_rows(row):
        return jnp.broadcast_to(row, wide)

    for first in range(0, count, PANEL // 8):
        after = first + PANEL // 8
        cols = [
            [jnp.broadcast_to(tiles[u][:, 8 * first + c : 8 * first + c + 1], wide) for u in range(first, count)]
            for c in range(PANEL)
        ]
        for t in range(first, after):
            spread_ref[PANEL + t - first] = tiles[t]
        spread_ref[0] = cols[0][0]
        for t in range(1, PANEL // 8):
            spread_ref[PANEL + PANEL // 8 + t - 1] = cols[0][t]
        rows = [over_rows(spread_ref[PANEL + i // 8, i % 8 : i % 8 + 1, :]) for i in range(PANEL)]
        pivots, scaled = [], []
        for c in range(PANEL):
            def at(i):
                if c == 0:
                    slot = 0 if i < 8 else PANEL + PANEL // 8 + i // 8 - 1
                    return over_rows(spread_ref[slot, i % 8 : i % 8 + 1, :])
                return over_rows(cols[c][i // 8][i % 8 : i % 8 + 1, :])

            pivots.append(at(c))
            inverse = 1.0 / pivots[c]
            for k in range(c + 1, PANEL):
                factor = at(k) * inverse
                for u in range(k // 8, count - first):
                    cols[k][u] = cols[k][u] - factor * cols[c][u]
                rows[k] = rows[k] - factor * rows[c]
            scaled.append(rows[c] * inverse)
        for u in range(after, count):
            change = cols[0][u - first] * scaled[0]
            for c in range(1, PANEL):
                change = change + cols[c][u - first] * scaled[c]
            tiles[u] = tiles[u] - change
        for c in range(PANEL):
            t = first + c // 8
            tiles[t] = jnp.where(row_of == c % 8, rows[c] * lax.rsqrt(pivots[c]), tiles[t])
    return jnp.concatenate(tiles, axis=0)[:, size:]


def inverse_cholesky(m_ref, v_ref, spread_ref):
    size = m_ref.shape[0]
    v_ref[...] = jnp.zeros_like(v_ref)
    corner = m_ref[:BLOCK, :BLOCK]
    for lo in range(0, size, BLOCK):
        hi = lo + BLOCK
        end = min(hi + BLOCK, size)
        inner = inverse_factor(corner, spread_ref)
        if hi < size:
            across = contract(inner, m_ref[lo:hi, hi:end], 1, 0)
            down = contract(m_ref[hi:end, lo:hi], inner, 1, 1)
            corner = m_ref[hi:end, hi:end] - contract(down, across, 1, 0)
        if lo:
            v_ref[lo:hi, :lo] = contract(inner, v_ref[lo:hi, :lo], 1, 0)
        v_ref[lo:hi, lo:hi] = inner
        if end < size:
            far_across = contract(inner, m_ref[lo:hi, end:], 1, 0)
            far_down = contract(m_ref[end:, lo:hi], inner, 1, 1)
            m_ref[hi:end, end:] -= contract(down, far_across, 1, 0)
            m_ref[end:, hi:end] -= contract(far_down, across, 1, 0)
            m_ref[end:, end:] -= contract(far_down, far_across, 1, 0)
            v_ref[end:, :hi] -= contract(far_down, v_ref[lo:hi, :hi], 1, 0)
        if hi < size:
            v_ref[hi:end, :hi] -= contract(down, v_ref[lo:hi, :hi], 1, 0)


def offsets_at(side, distance):
    order = []
    for dx in range(side):
        for dz in range(side):
            if min(dx, side - dx) + min(dz, side - dz) != distance:
                continue
            back_x, back_z = (side - dx) % side, (side - dz) % side
            for offset in ((dx, dz), (back_x, back_z), (dz, back_x), (back_z, dx)):
                if offset not in order:
                    order.append(offset)
    return order


def late_offsets(side):
    return [(offset, 0) for offset in offsets_at(side, 3)]


def raw_offsets(side):
    every = [(offset, flip) for d in (4, 3, 2, 1) for offset in offsets_at(side, d) for flip in range(2)]
    return [(offset, flip) for offset, flip in every if (offset, flip) not in late_offsets(side)]


def halves_of(x):
    high = x.astype(jnp.bfloat16)
    return high, (x - high.astype(jnp.float32)).astype(jnp.bfloat16)


def three_products(x, across):
    high, low = halves_of(x)
    return jnp.concatenate([high, low, high] if across else [high, high, low], axis=1)


def truncate(
    side,
    scale,
    slab_ref,
    start_ref,
    moved,
    rows_ref,
    v_ref,
    slab,
    acc,
    part,
    pair,
    mine,
    first_in,
    partial,
    second_in,
    line,
    whole,
    start_held,
    product_ref,
    m_ref,
    spread_ref,
    late_rows,
    late_out,
    load_sem,
    own_sem,
    late_sem,
    sum_send,
    sum_recv,
    row_send,
    row_recv,
):
    y, x, z, core = (lax.axis_index(name) for name in AXES)
    rank, columns = rows_ref.shape
    tiles = columns // TILE
    blocks = [(i, j) for i in range(tiles) for j in range(i, tiles)]
    half = len(blocks) // 2
    count = slab_ref.shape[0]
    held = moved.shape[0]
    depth = count // CHUNKS
    wide = TILE // side
    thin = wide // side

    loads = [
        pltpu.make_async_copy(slab_ref.at[pl.ds(n * depth, depth)], slab.at[n], load_sem.at[n]) for n in range(CHUNKS)
    ]
    loads.append(pltpu.make_async_copy(start_ref, start_held, load_sem.at[CHUNKS]))
    for load in loads:
        load.start()

    first, second = x + core * (z - x), z + core * (x - z)

    def in_plane(f, s):
        return f + core * (s - f), s + core * (f - s)

    steps = range(1, side)
    along_first = [(y, *in_plane(lax.rem(first + k, side), second), core) for k in steps]
    along_second = [(y, *in_plane(first, lax.rem(second + k, side)), core) for k in steps]
    along_y = [(lax.rem(y + k, side), x, z, core) for k in steps]
    partner = (y, x, z, 1 - core)

    barrier = pltpu.get_barrier_semaphore()
    greeted = [*along_first, *along_second, *along_y, partner]
    for to in greeted:
        pl.semaphore_signal(barrier, inc=1, device_id=dict(zip(AXES, to)), device_id_type=MESH)

    def rows_of(index, size):
        return pl.ds(pl.multiple_of(index * size, size), size)

    def number(to):
        return (to[1] * side + to[2]) * 2 + to[3]

    me = number((y, x, z, core))

    def chip(offset):
        step_x, step_z = (step + core * ((side - step) % side - step) for step in offset)
        return lax.rem(x + step_x, side), lax.rem(z + step_z, side)

    def devices(offsets):
        return [(y, *chip(offset), core + flip * (1 - 2 * core)) for offset, flip in offsets]

    groups = {"near": [partner], "early": devices(raw_offsets(side)[:2]), "raw": devices(raw_offsets(side)[2:]), "late": devices(late_offsets(side))}
    exchange, kept, late = {}, [], []
    slot = 0
    for name, peers in groups.items():
        exchange[name] = []
        for n, to in enumerate(peers):
            for i in range(held):
                point = number(to) * held + i
                src, dst = slab_ref.at[:, point, :], moved.at[i, rows_of(me, count), :]
                if name == "late":
                    place = pl.ds((n * held + i) * count, count)
                    late.append(pltpu.make_async_copy(src, late_rows.at[place], late_sem.at[n, i]))
                    src, dst = late_out.at[place], moved.at[i, rows_of(me, count), pl.ds(0, rank)]
                exchange[name].append(
                    pltpu.make_async_remote_copy(
                        src_ref=src,
                        dst_ref=dst,
                        send_sem=row_send.at[slot, i],
                        recv_sem=row_recv.at[slot, i],
                        device_id=dict(zip(AXES, to)),
                        device_id_type=MESH,
                    )
                )
            slot += 1
    for i in range(held):
        kept.append(
            pltpu.make_async_copy(slab_ref.at[:, me * held + i, :], moved.at[i, rows_of(me, count), :], own_sem.at[i])
        )

    def start(copies):
        for copy in copies:
            copy.start()

    for n in range(CHUNKS):
        loads[n].wait()
        high, low = halves_of(slab[n].reshape(-1, columns))
        for left, right, rows, lo in (
            (high[:, :256], high[:, :256], 256, 0),
            (high, high[:, 256:], columns, 256),
            (high, low, columns, columns),
        ):
            new = lax.dot_general(left, right, (((0,), (0,)), ((), ())), preferred_element_type=jnp.float32)
            place = (slice(0, rows), slice(lo, lo + new.shape[1]))
            acc[place] = acc[place] + new if n else new
    for n, (i, j) in enumerate(blocks):
        across = acc[i * TILE : (i + 1) * TILE, columns + j * TILE : columns + (j + 1) * TILE]
        down = acc[j * TILE : (j + 1) * TILE, columns + i * TILE : columns + (i + 1) * TILE]
        part[n] = (acc[i * TILE : (i + 1) * TILE, j * TILE : (j + 1) * TILE] + (across + down.T)) * scale
    pl.semaphore_wait(barrier, len(greeted))

    sent = []

    def send(src, dst, to):
        slot = len(sent)
        sent.append(
            pltpu.make_async_remote_copy(
                src_ref=src,
                dst_ref=dst,
                send_sem=sum_send.at[slot],
                recv_sem=sum_recv.at[slot],
                device_id=dict(zip(AXES, to)),
                device_id_type=MESH,
            )
        )
        sent[slot].start()
        return sent[slot]

    def arrive(copies):
        for copy in copies:
            copy.wait_recv()

    def wait(copies):
        for copy in copies:
            copy.wait()

    arrive([send(part.at[pl.ds((1 - core) * half, half)], pair, partner)])
    own_half = pl.ds(core * half, half)
    mine[...] = part[own_half] + pair[...]

    copies = [
        send(mine.at[:, rows_of(lax.rem(first + k, side), wide), :], first_in.at[k - 1], to)
        for k, to in zip(steps, along_first)
    ]
    start(kept + exchange["near"] + late)
    arrive(copies)
    partial[...] = mine[:, rows_of(first, wide), :] + (first_in[0] + sum(first_in[k] for k in range(1, side - 1)))
    copies = [
        send(partial.at[:, rows_of(lax.rem(second + k, side), thin), :], second_in.at[k - 1], to)
        for k, to in zip(steps, along_second)
    ]
    arrive(copies)
    line[y] = partial[:, rows_of(second, thin), :] + (second_in[0] + sum(second_in[k] for k in range(1, side - 1)))
    copies = [send(line.at[y], line.at[y], to) for to in along_y]
    start(exchange["early"])
    arrive(copies)
    total = line[0]
    for k in steps:
        total = total + line[k]
    own = whole.at[own_half, rows_of(first * side + second, thin), :]
    own[...] = total

    arrive([send(own, own, to) for to in along_second])

    def strip(f):
        return whole.at[own_half, rows_of(f, wide), :]

    copies = [send(strip(first), strip(first), to) for to in along_first]
    passed = [send(strip(first), strip(first), partner)]
    for k, copy in zip(steps, copies):
        copy.wait_recv()
        piece = strip(lax.rem(first + side - k, side))
        passed.append(send(piece, piece, partner))
    start(exchange["raw"])
    arrive(passed)

    for n, (i, j) in enumerate(blocks):
        block = whole[n]
        acc[i * TILE : (i + 1) * TILE, j * TILE : (j + 1) * TILE] = block
        if i != j:
            acc[j * TILE : (j + 1) * TILE, i * TILE : (i + 1) * TILE] = block.T
    loads[CHUNKS].wait()
    rows_ref[...] = start_held[...].T

    def step(k, carry):
        product_ref[...] = contract(rows_ref[...], acc[:, :columns], 1, 0)

        @pl.when(k == ITERS - 1)
        def _():
            wait(late)
            late_out[...] = short_contract(late_rows[...], product_ref[...], 1, 1)
            start(exchange["late"])

        def either(out_ref, a_ref, b_ref, dim_b):
            @pl.when(k == 0)
            def _():
                out_ref[...] = contract(a_ref[...], b_ref[...], 1, dim_b)

            @pl.when(k > 0)
            def _():
                out_ref[...] = short_contract(a_ref[...], b_ref[...], 1, dim_b)

        either(m_ref, product_ref, product_ref, 1)
        inverse_cholesky(m_ref, v_ref, spread_ref)
        either(rows_ref, v_ref, product_ref, 0)
        return carry

    lax.fori_loop(0, ITERS, step, 0)
    for copies in exchange.values():
        wait(copies)
    wait(kept)
    for copy in sent:
        copy.wait_send()


def project(side, moved_ref, rows_ref, v_ref, out_ref, basis_ref, staged, turned, store_sem):
    x, z, core = (lax.axis_index(name) for name in DEV)
    held, count, rank = staged.shape
    turned[...] = rows_ref[...].T
    stores = [pltpu.make_async_copy(turned, basis_ref, store_sem.at[0])]
    stores[0].start()
    basis = three_products(rows_ref[...], True)
    stripes = [(i, pl.ds(lo, STRIPE)) for i in range(held) for lo in range(0, count, STRIPE)]
    for i, rows in stripes:
        staged[i, rows, :] = lax.dot_general(
            three_products(moved_ref[i, rows, :], False),
            basis,
            (((1,), (1,)), ((), ())),
            preferred_element_type=jnp.float32,
        )
    size = count // (2 * side * side)
    places = []
    for (dx, dz), flip in late_offsets(side):
        chip = lax.rem(x + dx, side) * side + lax.rem(z + dz, side)
        device = 2 * chip + core + flip * (1 - 2 * core)
        places += [(i, pl.ds(pl.multiple_of(device * size, size), size)) for i in range(held)]
    late = jnp.concatenate([moved_ref[i, rows, :rank] for i, rows in places], axis=0)
    late = short_contract(late, v_ref[...], 1, 1)
    for n, (i, rows) in enumerate(places):
        staged[i, rows, :] = late[n * size : (n + 1) * size]
    for n, (i, rows) in enumerate(stripes):
        stores.append(pltpu.make_async_copy(staged.at[i, rows, :], out_ref.at[i, rows, :], store_sem.at[n + 1]))
        stores[-1].start()
    for store in stores:
        store.wait()


def on_device(slab, start):
    count, points, columns = slab.shape
    rank = start.shape[1]
    side = lax.axis_size("grp")
    peers = lax.axis_size(DEV)
    held = points // peers
    scale = 1.0 / (count * points * side * peers)
    tiles = columns // TILE
    half = tiles * (tiles + 1) // 4
    late = len(late_offsets(side))
    slots = 1 + 5 * (side - 1) + side
    vmem = pl.BlockSpec(memory_space=pltpu.VMEM)
    hbm = pl.BlockSpec(memory_space=pltpu.HBM)

    def scratch(*shape):
        return pltpu.VMEM(shape, jnp.float32)

    moved, rows, factor = pl.pallas_call(
        functools.partial(truncate, side, scale),
        out_shape=(
            jax.ShapeDtypeStruct((held, count * peers, columns), jnp.float32),
            jax.ShapeDtypeStruct((rank, columns), jnp.float32),
            jax.ShapeDtypeStruct((rank, rank), jnp.float32),
        ),
        in_specs=[hbm, hbm],
        out_specs=(vmem, vmem, vmem),
        scratch_shapes=[
            scratch(CHUNKS, count // CHUNKS, points, columns),
            scratch(columns, 2 * columns),
            scratch(2 * half, TILE, TILE),
            scratch(half, TILE, TILE),
            scratch(half, TILE, TILE),
            scratch(side - 1, half, TILE // side, TILE),
            scratch(half, TILE // side, TILE),
            scratch(side - 1, half, TILE // side**2, TILE),
            scratch(side, half, TILE // side**2, TILE),
            scratch(2 * half, TILE, TILE),
            scratch(columns, rank),
            scratch(rank, columns),
            scratch(rank, rank),
            scratch(PANEL + PANEL // 4, 8, 2 * BLOCK),
            scratch(late * held * count, columns),
            scratch(late * held * count, rank),
            pltpu.SemaphoreType.DMA((CHUNKS + 1,)),
            pltpu.SemaphoreType.DMA((held,)),
            pltpu.SemaphoreType.DMA((late, held)),
            pltpu.SemaphoreType.DMA((slots,)),
            pltpu.SemaphoreType.DMA((slots,)),
            pltpu.SemaphoreType.DMA((peers - 1, held)),
            pltpu.SemaphoreType.DMA((peers - 1, held)),
        ],
        compiler_params=pltpu.CompilerParams(
            collective_id=0, has_side_effects=True, vmem_limit_bytes=47 * 1024 * 1024
        ),
        name="truncate",
    )(slab, start)
    return pl.pallas_call(
        functools.partial(project, side),
        out_shape=(
            jax.ShapeDtypeStruct((held, count * peers, rank), jnp.float32),
            jax.ShapeDtypeStruct((columns, rank), jnp.float32),
        ),
        in_specs=[vmem, vmem, vmem],
        out_specs=(hbm, hbm),
        scratch_shapes=[
            scratch(held, count * peers, rank),
            scratch(columns, rank),
            pltpu.SemaphoreType.DMA((1 + held * count * peers // STRIPE,)),
        ],
        compiler_params=pltpu.CompilerParams(vmem_limit_bytes=24 * 1024 * 1024),
        name="project",
    )(moved, rows, factor)


def solution(mesh):
    torus = Mesh(mesh.devices.reshape(mesh.shape["grp"], 4, 4, 2), AXES)
    return jax.shard_map(
        on_device,
        mesh=torus,
        in_specs=(P(AXES, None, None), P()),
        out_specs=(P(DEV, "grp", None), P()),
        check_vma=False,
    )
```

```python
import functools

import jax
import jax.numpy as jnp
from jax import lax
from jax.experimental import pallas as pl
from jax.experimental.pallas import tpu as pltpu
from jax.sharding import Mesh
from jax.sharding import PartitionSpec as P

ITERS = 4
DEV = ("dev_0", "dev_1", "dev_2")
AXES = ("grp", *DEV)
MESH = pl.DeviceIdType.MESH
HIGHEST = lax.Precision.HIGHEST
BLOCK = 64
PANEL = 16
TILE = 128
CHUNKS = 4
STRIPE = 256


def short_contract(a, b, dim_a, dim_b):
    (a, a_low), (b, b_low) = halves_of(a), halves_of(b)
    dims = (((dim_a,), (dim_b,)), ((), ()))
    products = [lax.dot_general(p, q, dims, preferred_element_type=jnp.float32) for p, q in ((a, b), (a, b_low), (a_low, b))]
    return products[0] + (products[1] + products[2])


def contract(a, b, dim_a, dim_b):
    return lax.dot_general(
        a, b, (((dim_a,), (dim_b,)), ((), ())), precision=HIGHEST, preferred_element_type=jnp.float32
    )


def inverse_factor(block, spread_ref):
    size = block.shape[0]
    diagonal = lax.broadcasted_iota(jnp.int32, (size, size), 0) == lax.broadcasted_iota(jnp.int32, (size, size), 1)
    both = jnp.concatenate([block, diagonal.astype(jnp.float32)], axis=1)
    wide = (8, 2 * size)
    count = size // 8
    tiles = [both[8 * t : 8 * t + 8, :] for t in range(count)]
    row_of = lax.broadcasted_iota(jnp.int32, wide, 0)

    def over_rows(row):
        return jnp.broadcast_to(row, wide)

    for first in range(0, count, PANEL // 8):
        after = first + PANEL // 8
        cols = [
            [jnp.broadcast_to(tiles[u][:, 8 * first + c : 8 * first + c + 1], wide) for u in range(first, count)]
            for c in range(PANEL)
        ]
        for t in range(first, after):
            spread_ref[PANEL + t - first] = tiles[t]
        spread_ref[0] = cols[0][0]
        for t in range(1, PANEL // 8):
            spread_ref[PANEL + PANEL // 8 + t - 1] = cols[0][t]
        rows = [over_rows(spread_ref[PANEL + i // 8, i % 8 : i % 8 + 1, :]) for i in range(PANEL)]
        pivots, scaled = [], []
        for c in range(PANEL):
            def at(i):
                if c == 0:
                    slot = 0 if i < 8 else PANEL + PANEL // 8 + i // 8 - 1
                    return over_rows(spread_ref[slot, i % 8 : i % 8 + 1, :])
                return over_rows(cols[c][i // 8][i % 8 : i % 8 + 1, :])

            pivots.append(at(c))
            inverse = 1.0 / pivots[c]
            for k in range(c + 1, PANEL):
                factor = at(k) * inverse
                for u in range(k // 8, count - first):
                    cols[k][u] = cols[k][u] - factor * cols[c][u]
                rows[k] = rows[k] - factor * rows[c]
            scaled.append(rows[c] * inverse)
        for u in range(after, count):
            change = cols[0][u - first] * scaled[0]
            for c in range(1, PANEL):
                change = change + cols[c][u - first] * scaled[c]
            tiles[u] = tiles[u] - change
        for c in range(PANEL):
            t = first + c // 8
            tiles[t] = jnp.where(row_of == c % 8, rows[c] * lax.rsqrt(pivots[c]), tiles[t])
    return jnp.concatenate(tiles, axis=0)[:, size:]


def inverse_cholesky(m_ref, v_ref, spread_ref, contract):
    size = m_ref.shape[0]
    v_ref[...] = jnp.zeros_like(v_ref)
    corner = m_ref[:BLOCK, :BLOCK]
    for lo in range(0, size, BLOCK):
        hi = lo + BLOCK
        end = min(hi + BLOCK, size)
        inner = inverse_factor(corner, spread_ref)
        if hi < size:
            across = contract(inner, m_ref[lo:hi, hi:end], 1, 0)
            down = contract(m_ref[hi:end, lo:hi], inner, 1, 1)
            corner = m_ref[hi:end, hi:end] - contract(down, across, 1, 0)
        if lo:
            v_ref[lo:hi, :lo] = contract(inner, v_ref[lo:hi, :lo], 1, 0)
        v_ref[lo:hi, lo:hi] = inner
        if end < size:
            far_across = contract(inner, m_ref[lo:hi, end:], 1, 0)
            far_down = contract(m_ref[end:, lo:hi], inner, 1, 1)
            m_ref[hi:end, end:] -= contract(down, far_across, 1, 0)
            m_ref[end:, hi:end] -= contract(far_down, across, 1, 0)
            m_ref[end:, end:] -= contract(far_down, far_across, 1, 0)
            v_ref[end:, :hi] -= contract(far_down, v_ref[lo:hi, :hi], 1, 0)
        if hi < size:
            v_ref[hi:end, :hi] -= contract(down, v_ref[lo:hi, :hi], 1, 0)


def offsets_at(side, distance):
    order = []
    for dx in range(side):
        for dz in range(side):
            if min(dx, side - dx) + min(dz, side - dz) != distance:
                continue
            back_x, back_z = (side - dx) % side, (side - dz) % side
            for offset in ((dx, dz), (back_x, back_z), (dz, back_x), (back_z, dx)):
                if offset not in order:
                    order.append(offset)
    return order


def late_offsets(side):
    return [(offset, 0) for offset in offsets_at(side, 3)]


def raw_offsets(side):
    every = [(offset, flip) for d in (4, 3, 2, 1) for offset in offsets_at(side, d) for flip in range(2)]
    return [(offset, flip) for offset, flip in every if (offset, flip) not in late_offsets(side)]


def halves_of(x):
    high = x.astype(jnp.bfloat16)
    return high, (x - high.astype(jnp.float32)).astype(jnp.bfloat16)


def three_products(x, across):
    high, low = halves_of(x)
    return jnp.concatenate([high, low, high] if across else [high, high, low], axis=1)


def truncate(
    side,
    scale,
    slab_ref,
    start_ref,
    moved,
    rows_ref,
    v_ref,
    slab,
    acc,
    part,
    pair,
    mine,
    first_in,
    partial,
    second_in,
    line,
    whole,
    start_held,
    product_ref,
    m_ref,
    spread_ref,
    late_rows,
    late_out,
    load_sem,
    own_sem,
    late_sem,
    sum_send,
    sum_recv,
    row_send,
    row_recv,
):
    y, x, z, core = (lax.axis_index(name) for name in AXES)
    rank, columns = rows_ref.shape
    tiles = columns // TILE
    blocks = [(i, j) for i in range(tiles) for j in range(i, tiles)]
    half = len(blocks) // 2
    count = slab_ref.shape[0]
    held = moved.shape[0]
    depth = count // CHUNKS
    wide = TILE // side
    thin = wide // side

    loads = [
        pltpu.make_async_copy(slab_ref.at[pl.ds(n * depth, depth)], slab.at[n], load_sem.at[n]) for n in range(CHUNKS)
    ]
    loads.append(pltpu.make_async_copy(start_ref, start_held, load_sem.at[CHUNKS]))
    for load in loads:
        load.start()

    first, second = x + core * (z - x), z + core * (x - z)

    def in_plane(f, s):
        return f + core * (s - f), s + core * (f - s)

    steps = range(1, side)
    along_first = [(y, *in_plane(lax.rem(first + k, side), second), core) for k in steps]
    along_second = [(y, *in_plane(first, lax.rem(second + k, side)), core) for k in steps]
    along_y = [(lax.rem(y + k, side), x, z, core) for k in steps]
    partner = (y, x, z, 1 - core)

    barrier = pltpu.get_barrier_semaphore()
    greeted = [*along_first, *along_second, *along_y, partner]
    for to in greeted:
        pl.semaphore_signal(barrier, inc=1, device_id=dict(zip(AXES, to)), device_id_type=MESH)

    def rows_of(index, size):
        return pl.ds(pl.multiple_of(index * size, size), size)

    def number(to):
        return (to[1] * side + to[2]) * 2 + to[3]

    me = number((y, x, z, core))

    def chip(offset):
        step_x, step_z = (step + core * ((side - step) % side - step) for step in offset)
        return lax.rem(x + step_x, side), lax.rem(z + step_z, side)

    def devices(offsets):
        return [(y, *chip(offset), core + flip * (1 - 2 * core)) for offset, flip in offsets]

    groups = {"near": [partner], "early": devices(raw_offsets(side)[:2]), "raw": devices(raw_offsets(side)[2:]), "late": devices(late_offsets(side))}
    exchange, kept, late = {}, [], []
    slot = 0
    for name, peers in groups.items():
        exchange[name] = []
        for n, to in enumerate(peers):
            for i in range(held):
                point = number(to) * held + i
                src, dst = slab_ref.at[:, point, :], moved.at[i, rows_of(me, count), :]
                if name == "late":
                    place = pl.ds((n * held + i) * count, count)
                    late.append(pltpu.make_async_copy(src, late_rows.at[place], late_sem.at[n, i]))
                    src, dst = late_out.at[place], moved.at[i, rows_of(me, count), pl.ds(0, rank)]
                exchange[name].append(
                    pltpu.make_async_remote_copy(
                        src_ref=src,
                        dst_ref=dst,
                        send_sem=row_send.at[slot, i],
                        recv_sem=row_recv.at[slot, i],
                        device_id=dict(zip(AXES, to)),
                        device_id_type=MESH,
                    )
                )
            slot += 1
    for i in range(held):
        kept.append(
            pltpu.make_async_copy(slab_ref.at[:, me * held + i, :], moved.at[i, rows_of(me, count), :], own_sem.at[i])
        )

    def start(copies):
        for copy in copies:
            copy.start()

    for n in range(CHUNKS):
        loads[n].wait()
        high, low = halves_of(slab[n].reshape(-1, columns))
        for left, right, rows, lo in (
            (high[:, :256], high[:, :256], 256, 0),
            (high, high[:, 256:], columns, 256),
            (high, low, columns, columns),
        ):
            new = lax.dot_general(left, right, (((0,), (0,)), ((), ())), preferred_element_type=jnp.float32)
            place = (slice(0, rows), slice(lo, lo + new.shape[1]))
            acc[place] = acc[place] + new if n else new
    for n, (i, j) in enumerate(blocks):
        across = acc[i * TILE : (i + 1) * TILE, columns + j * TILE : columns + (j + 1) * TILE]
        down = acc[j * TILE : (j + 1) * TILE, columns + i * TILE : columns + (i + 1) * TILE]
        part[n] = (acc[i * TILE : (i + 1) * TILE, j * TILE : (j + 1) * TILE] + (across + down.T)) * scale
    pl.semaphore_wait(barrier, len(greeted))

    sent = []

    def send(src, dst, to):
        slot = len(sent)
        sent.append(
            pltpu.make_async_remote_copy(
                src_ref=src,
                dst_ref=dst,
                send_sem=sum_send.at[slot],
                recv_sem=sum_recv.at[slot],
                device_id=dict(zip(AXES, to)),
                device_id_type=MESH,
            )
        )
        sent[slot].start()
        return sent[slot]

    def arrive(copies):
        for copy in copies:
            copy.wait_recv()

    def wait(copies):
        for copy in copies:
            copy.wait()

    arrive([send(part.at[pl.ds((1 - core) * half, half)], pair, partner)])
    own_half = pl.ds(core * half, half)
    mine[...] = part[own_half] + pair[...]

    copies = [
        send(mine.at[:, rows_of(lax.rem(first + k, side), wide), :], first_in.at[k - 1], to)
        for k, to in zip(steps, along_first)
    ]
    start(kept + exchange["near"] + late)
    arrive(copies)
    partial[...] = mine[:, rows_of(first, wide), :] + (first_in[0] + sum(first_in[k] for k in range(1, side - 1)))
    copies = [
        send(partial.at[:, rows_of(lax.rem(second + k, side), thin), :], second_in.at[k - 1], to)
        for k, to in zip(steps, along_second)
    ]
    arrive(copies)
    line[y] = partial[:, rows_of(second, thin), :] + (second_in[0] + sum(second_in[k] for k in range(1, side - 1)))
    copies = [send(line.at[y], line.at[y], to) for to in along_y]
    start(exchange["early"])
    arrive(copies)
    total = line[0]
    for k in steps:
        total = total + line[k]
    own = whole.at[own_half, rows_of(first * side + second, thin), :]
    own[...] = total

    arrive([send(own, own, to) for to in along_second])

    def strip(f):
        return whole.at[own_half, rows_of(f, wide), :]

    copies = [send(strip(first), strip(first), to) for to in along_first]
    passed = [send(strip(first), strip(first), partner)]
    for k, copy in zip(steps, copies):
        copy.wait_recv()
        piece = strip(lax.rem(first + side - k, side))
        passed.append(send(piece, piece, partner))
    start(exchange["raw"])
    arrive(passed)

    for n, (i, j) in enumerate(blocks):
        block = whole[n]
        acc[i * TILE : (i + 1) * TILE, j * TILE : (j + 1) * TILE] = block
        if i != j:
            acc[j * TILE : (j + 1) * TILE, i * TILE : (i + 1) * TILE] = block.T
    loads[CHUNKS].wait()
    rows_ref[...] = start_held[...].T

    def step(k, carry):
        product_ref[...] = contract(rows_ref[...], acc[:, :columns], 1, 0)

        @pl.when(k == ITERS - 1)
        def _():
            wait(late)
            late_out[...] = short_contract(late_rows[...], product_ref[...], 1, 1)
            start(exchange["late"])

        def orthonormalise(product):
            m_ref[...] = product(product_ref[...], product_ref[...], 1, 1)
            inverse_cholesky(m_ref, v_ref, spread_ref, product)
            rows_ref[...] = product(v_ref[...], product_ref[...], 1, 0)

        pl.when(k == 0)(functools.partial(orthonormalise, contract))
        pl.when(k > 0)(functools.partial(orthonormalise, short_contract))
        return carry

    lax.fori_loop(0, ITERS, step, 0)
    for copies in exchange.values():
        wait(copies)
    wait(kept)
    for copy in sent:
        copy.wait_send()


def project(side, moved_ref, rows_ref, v_ref, out_ref, basis_ref, staged, turned, store_sem):
    x, z, core = (lax.axis_index(name) for name in DEV)
    held, count, rank = staged.shape
    turned[...] = rows_ref[...].T
    stores = [pltpu.make_async_copy(turned, basis_ref, store_sem.at[0])]
    stores[0].start()
    basis = three_products(rows_ref[...], True)
    stripes = [(i, pl.ds(lo, STRIPE)) for i in range(held) for lo in range(0, count, STRIPE)]
    for i, rows in stripes:
        staged[i, rows, :] = lax.dot_general(
            three_products(moved_ref[i, rows, :], False),
            basis,
            (((1,), (1,)), ((), ())),
            preferred_element_type=jnp.float32,
        )
    size = count // (2 * side * side)
    places = []
    for (dx, dz), flip in late_offsets(side):
        chip = lax.rem(x + dx, side) * side + lax.rem(z + dz, side)
        device = 2 * chip + core + flip * (1 - 2 * core)
        places += [(i, pl.ds(pl.multiple_of(device * size, size), size)) for i in range(held)]
    late = jnp.concatenate([moved_ref[i, rows, :rank] for i, rows in places], axis=0)
    late = short_contract(late, v_ref[...], 1, 1)
    for n, (i, rows) in enumerate(places):
        staged[i, rows, :] = late[n * size : (n + 1) * size]
    for n, (i, rows) in enumerate(stripes):
        stores.append(pltpu.make_async_copy(staged.at[i, rows, :], out_ref.at[i, rows, :], store_sem.at[n + 1]))
        stores[-1].start()
    for store in stores:
        store.wait()


def on_device(slab, start):
    count, points, columns = slab.shape
    rank = start.shape[1]
    side = lax.axis_size("grp")
    peers = lax.axis_size(DEV)
    held = points // peers
    scale = 1.0 / (count * points * side * peers)
    tiles = columns // TILE
    half = tiles * (tiles + 1) // 4
    late = len(late_offsets(side))
    slots = 1 + 5 * (side - 1) + side
    vmem = pl.BlockSpec(memory_space=pltpu.VMEM)
    hbm = pl.BlockSpec(memory_space=pltpu.HBM)

    def scratch(*shape):
        return pltpu.VMEM(shape, jnp.float32)

    moved, rows, factor = pl.pallas_call(
        functools.partial(truncate, side, scale),
        out_shape=(
            jax.ShapeDtypeStruct((held, count * peers, columns), jnp.float32),
            jax.ShapeDtypeStruct((rank, columns), jnp.float32),
            jax.ShapeDtypeStruct((rank, rank), jnp.float32),
        ),
        in_specs=[hbm, hbm],
        out_specs=(vmem, vmem, vmem),
        scratch_shapes=[
            scratch(CHUNKS, count // CHUNKS, points, columns),
            scratch(columns, 2 * columns),
            scratch(2 * half, TILE, TILE),
            scratch(half, TILE, TILE),
            scratch(half, TILE, TILE),
            scratch(side - 1, half, TILE // side, TILE),
            scratch(half, TILE // side, TILE),
            scratch(side - 1, half, TILE // side**2, TILE),
            scratch(side, half, TILE // side**2, TILE),
            scratch(2 * half, TILE, TILE),
            scratch(columns, rank),
            scratch(rank, columns),
            scratch(rank, rank),
            scratch(PANEL + PANEL // 4, 8, 2 * BLOCK),
            scratch(late * held * count, columns),
            scratch(late * held * count, rank),
            pltpu.SemaphoreType.DMA((CHUNKS + 1,)),
            pltpu.SemaphoreType.DMA((held,)),
            pltpu.SemaphoreType.DMA((late, held)),
            pltpu.SemaphoreType.DMA((slots,)),
            pltpu.SemaphoreType.DMA((slots,)),
            pltpu.SemaphoreType.DMA((peers - 1, held)),
            pltpu.SemaphoreType.DMA((peers - 1, held)),
        ],
        compiler_params=pltpu.CompilerParams(
            collective_id=0, has_side_effects=True, vmem_limit_bytes=47 * 1024 * 1024
        ),
        name="truncate",
    )(slab, start)
    return pl.pallas_call(
        functools.partial(project, side),
        out_shape=(
            jax.ShapeDtypeStruct((held, count * peers, rank), jnp.float32),
            jax.ShapeDtypeStruct((columns, rank), jnp.float32),
        ),
        in_specs=[vmem, vmem, vmem],
        out_specs=(hbm, hbm),
        scratch_shapes=[
            scratch(held, count * peers, rank),
            scratch(columns, rank),
            pltpu.SemaphoreType.DMA((1 + held * count * peers // STRIPE,)),
        ],
        compiler_params=pltpu.CompilerParams(vmem_limit_bytes=24 * 1024 * 1024),
        name="project",
    )(moved, rows, factor)


def solution(mesh):
    torus = Mesh(mesh.devices.reshape(mesh.shape["grp"], 4, 4, 2), AXES)
    return jax.shard_map(
        on_device,
        mesh=torus,
        in_specs=(P(AXES, None, None), P()),
        out_specs=(P(DEV, "grp", None), P()),
        check_vma=False,
    )
```
